128 devices in a mesh: row: 16 (over z, y), col: 8 (over x, core).
Axes of the slice: x: 4, y: 4, z: 4, core: 2. Of those that a mesh axis runs over, the one named last changes fastest.
Arguments:
- covariance: bfloat16 [28672, 28672], P('row', 'col'), may hold values from -1 to 8, as said below
- right_side: float32 [28672, 256], P(('col', 'row')), may hold values from -50 to 50
Outputs:
- solution: float32 [28672, 256], P(('col', 'row'))
- residual: float32 [28672, 256], P(('col', 'row'))
- direction: float32 [28672, 256], P(('col', 'row'))
The draws below stay inside these ranges and needn't reach their ends.
Inputs may be any that keep to these rules, and one draw needn't show every extreme that they name: `covariance`: symmetric and positive definite, with condition number under 100.
All inputs are finite; a program needn't handle non-finite values.
Results may differ from the reference program's by a relative error of at most 0.0158.
Values may be sent and summed in bfloat16 or wider, within the bound.
A program may use at most 128 MiB of HBM per device.

```python
import math
import jax
import jax.numpy as jnp
from jax import lax

ORDER = 28672
EDITS = 256
ITERS = 3


def draw_covariance(key, part):
    first_key, second_key = jax.random.split(jax.random.fold_in(key, 11))
    radius = 0.7
    top_scale = 4.0
    factor = radius / (2.0 * math.sqrt(2.0 * ORDER / 3.0))
    entries = jax.random.uniform(first_key, (ORDER, ORDER), jnp.float32, -1.0, 1.0)
    symmetric = (entries + entries.T) * factor
    positions = jnp.arange(ORDER)
    symmetric = symmetric.at[positions, positions].set(1.0)
    scales = jnp.sqrt(jnp.exp(jax.random.uniform(second_key, (ORDER,), jnp.float32, 0.0, math.log(top_scale))))
    return (symmetric * scales[:, None] * scales[None, :]).astype(jnp.bfloat16)


def draw_right_side(key, part):
    first_key, second_key = jax.random.split(jax.random.fold_in(key, 23), 2)
    row_pos = jnp.arange(ORDER).astype(jnp.float32) / ORDER
    row_scale = jnp.exp(math.log(10.0) * row_pos)
    col_scale = jnp.exp(jax.random.uniform(second_key, (EDITS,), jnp.float32, 0.0, math.log(10.0)))
    base_part = jax.random.normal(first_key, (ORDER, EDITS), jnp.float32)
    base_part = jnp.clip(base_part, -5.0, 5.0)
    return base_part * row_scale[:, None] * col_scale[None, :] * 0.1


def setup_inputs(seed: int = 0) -> dict:
    seeds = jax.random.split(jax.random.key(seed), 3)
    return {
        "covariance": draw_covariance(jax.random.fold_in(seeds[2], 71), 0),
        "right_side": draw_right_side(jax.random.fold_in(seeds[2], 71), 0),
    }


HIGHEST_PRECISION = lax.Precision.HIGHEST

def inner_product(left_block, right_block):
    return lax.dot_general(left_block.astype(jnp.float32), right_block.astype(jnp.float32), (((0,), (0,)), ((), ())), precision=HIGHEST_PRECISION, preferred_element_type=jnp.float32)

def apply_small(block, coeffs):
    return jnp.dot(block.astype(jnp.float32), coeffs.astype(jnp.float32), precision=HIGHEST_PRECISION, preferred_element_type=jnp.float32)

def symmetric_part(matrix):
    return 0.5 * (matrix + matrix.T)

def solve_spd(matrix, rhs_block):
    factor = jnp.linalg.cholesky(matrix)
    return jax.scipy.linalg.cho_solve((factor, True), rhs_block)

def covariance_times(covariance, lowered):
    strip_rows = math.gcd(ORDER, 1024)
    strips = covariance.reshape(ORDER // strip_rows, strip_rows, ORDER)
    widened = lowered.astype(jnp.float32)

    def one_strip(strip):
        return jnp.dot(strip.astype(jnp.float32), widened.astype(jnp.float32), precision=HIGHEST_PRECISION, preferred_element_type=jnp.float32)
    stacked = lax.map(one_strip, strips)
    return stacked.reshape(ORDER, EDITS)

def reference(covariance, right_side):
    solution = jnp.zeros_like(right_side)
    residual = right_side
    direction = right_side
    norm_now = inner_product(residual, residual)
    for iteration in range(ITERS):
        lowered = direction.astype(jnp.bfloat16)
        image = covariance_times(covariance, lowered)
        curvature = symmetric_part(inner_product(direction, image))
        alpha = solve_spd(curvature, norm_now)
        solution = solution + apply_small(direction, alpha)
        residual = residual - apply_small(image, alpha)
        norm_next = inner_product(residual, residual)
        beta = solve_spd(norm_now, norm_next)
        direction = residual + apply_small(direction, beta)
        norm_now = norm_next
    return (solution, residual, direction)
```

```python
import functools

import jax
import jax.numpy as jnp
from jax import lax
from jax.experimental import pallas as pl
from jax.experimental.pallas import tpu as pltpu
from jax.sharding import PartitionSpec as P

ITERS = 3
MESH = pl.DeviceIdType.MESH
HIGHEST = lax.Precision.HIGHEST
F32 = jnp.float32
BF16 = jnp.bfloat16
WIRE = jnp.bfloat16
SIDE = 256
HALF = SIDE // 2
RING = 4
OFFS = (0, -1, 1, 2)


def mm(left, right):
    return jnp.dot(left, right, precision=HIGHEST, preferred_element_type=F32)


def mm_t(left, right):
    return lax.dot_general(
        left, right, (((0,), (0,)), ((), ())), precision=HIGHEST, preferred_element_type=F32
    )


def gauss_jordan(mats, size):
    row = lax.broadcasted_iota(jnp.int32, (size, 1), 0)
    lane = lax.broadcasted_iota(jnp.int32, (1, size), 1)
    mats = list(mats)
    for k in range(size):
        for i, m in enumerate(mats):
            inv = 1.0 / m[k : k + 1, k : k + 1]
            pivot_row = jnp.where(lane == k, 1.0, m[k : k + 1, :]) * inv
            pivot_col = jnp.where(row == k, -1.0, m[:, k : k + 1])
            rest = jnp.where((row == k) | (lane == k), 0.0, m)
            mats[i] = rest - pivot_col * pivot_row
    return mats


def kernel(
    a_hbm, b_ref, x_ref, r_ref, d_ref,
    a, lb, part, s1, t1, s2, t2, s3, t3, rp, dp, qp, q,
    g, gt, g0, u1, g1, u2, g2, u3, h1, h0, gf, norm, full, inv, work, tri, small,
    a_sem, ag_send, ag_recv, rs_send, rs_recv, pm_send, pm_recv, ar_send, ar_recv,
):
    row, col = lax.axis_index("row"), lax.axis_index("col")
    z, y, x, core = row // RING, row % RING, col // 2, col % 2
    here = (x, y, z)

    def wrap(v):
        return (v + 2 * RING) % RING

    def device(pos, c):
        return (pos[2] * RING + pos[1], pos[0] * 2 + c)

    def along(axis, d):
        pos = list(here)
        pos[axis] = wrap(pos[axis] + d)
        return device(pos, core)

    other_core = device(here, 1 - core)

    def remote(src, dst, send, recv, target):
        return pltpu.make_async_remote_copy(
            src_ref=src, dst_ref=dst, send_sem=send, recv_sem=recv, device_id=target, device_id_type=MESH
        )

    load_a = pltpu.make_async_copy(a_hbm, a, a_sem)
    load_a.start()

    piece_out = col * 16 + row
    to_rows = (piece_out // 8, piece_out % 8)
    piece_in = row * 8 + col
    to_owner = (piece_in % 16, piece_in // 16)
    fixed = piece_out == piece_in

    barrier = pltpu.get_barrier_semaphore()

    def greet(target):
        pl.semaphore_signal(barrier, inc=1, device_id=target, device_id_type=MESH)

    for axis in range(3):
        for d in range(1, RING):
            greet(along(axis, d))
    greet(other_core)

    @pl.when(jnp.logical_not(fixed))
    def _():
        greet(to_rows)
        greet(to_owner)

    pl.semaphore_wait(barrier, jnp.where(fixed, 10, 12))

    def permute(src, dst, target, n):
        copy = remote(src, dst, pm_send.at[n], pm_recv.at[n], target)

        @pl.when(jnp.logical_not(fixed))
        def _():
            copy.start()

        @pl.when(fixed)
        def _():
            pltpu.make_async_copy(src, dst, pm_recv.at[n]).start()

        return copy

    def permute_wait(copy):
        copy.wait_recv()

        @pl.when(jnp.logical_not(fixed))
        def _():
            copy.wait_send()

    rows_in = permute(b_ref, rp, to_rows, 0)

    r_ref[...] = b_ref[...]
    d_ref[...] = b_ref[...]
    x_ref[...] = jnp.zeros_like(x_ref)

    def region(h, c1, c2, rows):
        zc, yc = (c2, c1) if h == 0 else (c1, c2)
        return lb.at[zc, yc, h, rows]

    def gather(h, g_, e, incoming):
        axes = (1, 2) if h == 0 else (2, 1)
        mine = (here[axes[0]], here[axes[1]])
        if incoming:
            off = (-1, 1, 2, 2)[e]
        else:
            off = (0, 0, -1, 1)[e]
        rows = (pl.ds(0, 112), pl.ds(0, 112), pl.ds(0, 64), pl.ds(64, 48))[e]
        if g_ == 0:
            c1, c2, axis = wrap(mine[0] + off), mine[1], axes[0]
        else:
            c1, c2, axis = wrap(mine[0] + OFFS[g_ - 1]), wrap(mine[1] + off), axes[1]
        ref = region(h, c1, c2, rows)
        n = h * 20 + g_ * 4 + e
        return remote(ref, ref, ag_send.at[n], ag_recv.at[n], along(axis, 1 if e % 2 == 0 else -1))

    def send(h, g_, *es):
        for e in es:
            gather(h, g_, e, False).start()

    def take(h, g_, *es):
        for e in es:
            gather(h, g_, e, True).wait_recv()

    def product(zc, j, first):
        cols = pl.ds(pl.multiple_of(zc * 896, 128), 896)
        block = lb[zc].reshape(896, SIDE)
        out = jnp.dot(a[j, :, cols], block, preferred_element_type=F32)
        if first:
            part[j] = out
        else:
            part[j] += out

    def all_products(zc, first):
        def body(j, carry):
            product(zc, j, first)
            return carry

        lax.fori_loop(0, 8, body, 0)

    def core_copy(i):
        return remote(s1.at[i], t1.at[i], rs_send.at[i], rs_recv.at[i], other_core)

    def ring_copy(src, dst, n, d):
        return remote(src, dst, rs_send.at[n], rs_recv.at[n], along(0, d))

    def reduce_copy(stage, m, d, src, dst):
        axis = (m + stage) % 3
        n = 2 + (stage * 3 + m) * 3 + d - 1
        return remote(src, dst, ar_send.at[n], ar_recv.at[n], along(axis, d))

    def spread_copy(stage, m, d, src, dst):
        axis = (m + stage) % 3
        n = 29 + (stage * 3 + m) * 3 + d - 1
        return remote(src, dst, ar_send.at[n], ar_recv.at[n], along(axis, d))

    def iteration(it, carry):
        lb[z, y] = d_ref[...].astype(BF16).reshape(2, 112, SIDE)
        for h in (0, 1):
            send(h, 0, 0, 1)
            send(h, 1, 0, 1)

        @pl.when(it > 0)
        def _():
            rp[...] = rp[...] - mm(qp[...], small[0])
            dp[...] = rp[...] + mm(dp[...], small[1])

        for h in (0, 1):
            take(h, 0, 0)
            send(h, 0, 2)
            send(h, 2, 0, 1)
        for h in (0, 1):
            take(h, 0, 1)
            send(h, 0, 3)
            send(h, 3, 0, 1)
        for h in (0, 1):
            take(h, 1, 0)
            send(h, 1, 2)
            take(h, 1, 1)
            send(h, 1, 3)
        for h in (0, 1):
            take(h, 0, 2, 3)
            send(h, 4, 0, 1)

        @pl.when(it == 0)
        def _():
            load_a.wait()

        for h in (0, 1):
            take(h, 2, 0)
            send(h, 2, 2)
            take(h, 2, 1)
            send(h, 2, 3)
        take(1, 1, 2, 3)
        all_products(z, True)
        for h in (0, 1):
            take(h, 3, 0)
            send(h, 3, 2)
            take(h, 3, 1)
            send(h, 3, 3)
        for h in (0, 1):
            take(h, 4, 0)
            send(h, 4, 2)
            take(h, 4, 1)
            send(h, 4, 3)
        take(1, 2, 2, 3)
        all_products(wrap(z - 1), False)
        take(1, 3, 2, 3)
        all_products(wrap(z + 1), False)
        take(1, 4, 2, 3)
        for g_ in (1, 2, 3, 4):
            take(0, g_, 2, 3)

        last = wrap(z + 2)

        def finish(i, c_):
            off = jnp.where(i == 0, 2, jnp.where(i == 1, 1, jnp.where(i == 2, 3, 0)))
            xc = (x + off) % RING
            j = 2 * xc + 1 - core
            product(last, j, False)
            s1[i] = part[j].astype(WIRE)
            core_copy(i).start()
            product(last, 2 * xc + core, False)
            return c_

        lax.fori_loop(0, 4, finish, 0)

        def chip_sum(i, off):
            core_copy(i).wait_recv()
            return part[2 * wrap(x + off) + core] + t1[i].astype(F32)

        far = chip_sum(0, 2)
        s2[0] = far[:112].astype(WIRE)
        s2[1] = far[112:].astype(WIRE)
        step = [
            ring_copy(s2.at[0], t2.at[0], 4, 1),
            ring_copy(s2.at[1], t2.at[1], 5, -1),
            ring_copy(s3.at[0], t3.at[0], 6, 1),
            ring_copy(s3.at[1], t3.at[1], 7, -1),
        ]
        step[0].start()
        step[1].start()
        right = chip_sum(1, 1)
        s3[0, 112:] = right[112:].astype(WIRE)
        step[0].wait_recv()
        s3[0, :112] = (right[:112] + t2[0].astype(F32)).astype(WIRE)
        step[2].start()
        left = chip_sum(2, -1)
        s3[1, :112] = left[:112].astype(WIRE)
        step[1].wait_recv()
        s3[1, 112:] = (left[112:] + t2[1].astype(F32)).astype(WIRE)
        step[3].start()
        own = chip_sum(3, 0)
        for h in (0, 1):
            for g_ in range(5):
                for e in range(4):
                    gather(h, g_, e, False).wait_send()
        step[2].wait_recv()
        step[3].wait_recv()
        qp[...] = own + t3[0].astype(F32) + t3[1].astype(F32)
        owner_in = permute(qp, q, to_owner, 1)

        @pl.when(it == 0)
        def _():
            permute_wait(rows_in)
            dp[...] = rp[...]

        image, res = qp[...], rp[...]
        g[0] = mm_t(dp[...], image)
        g[1] = mm_t(res, jnp.where(it == 0, res, image))
        g[2] = mm_t(image, image)
        theirs = pl.ds(pl.multiple_of((1 - core) * HALF, HALF), HALF)
        ours = pl.ds(pl.multiple_of(core * HALF, HALF), HALF)
        swap = remote(g.at[:, theirs], gt, ar_send.at[0], ar_recv.at[0], other_core)
        swap.start()
        for i in range(4):
            core_copy(i).wait_send()
        for c_ in step:
            c_.wait_send()
        swap.wait_recv()
        g0[...] = (g[:, ours] + gt[...]).reshape(3, RING, 32, SIDE)
        pending = [swap]

        def reduce_stage(stage, source, slots, result):
            for m in range(3):
                me = here[(m + stage) % 3]
                for d in (1, 3, 2):
                    src = source.at[m, wrap(me + d)] if stage < 2 else source.at[m]
                    copy = reduce_copy(stage, m, d, src, slots.at[m, me])
                    copy.start()
                    pending.append(copy)
                slots[m, me] = source[m, me] if stage < 2 else source[m]
            for m in range(3):
                me = here[(m + stage) % 3]
                for d in (1, 3, 2):
                    slot = slots.at[m, wrap(me - d)]
                    reduce_copy(stage, m, d, slot, slot).wait_recv()
                result(m, (slots[m, 0] + slots[m, 1]) + (slots[m, 2] + slots[m, 3]))

        def put1(m, v):
            g1[m] = v.reshape(RING, 8, SIDE)

        def put2(m, v):
            g2[m] = v

        def put3(m, v):
            h1[m, here[(m + 1) % 3]] = v

        reduce_stage(0, g0, u1, put1)
        reduce_stage(1, g1, u2, put2)
        reduce_stage(2, g2, u3, put3)
        for m in range(3):
            me = here[(m + 1) % 3]
            for d in (1, 3, 2):
                copy = spread_copy(1, m, d, h1.at[m, me], h1.at[m, me])
                copy.start()
                pending.append(copy)
        for m in range(3):
            me = here[(m + 1) % 3]
            for d in (1, 3, 2):
                slot = h1.at[m, wrap(me - d)]
                spread_copy(1, m, d, slot, slot).wait_recv()
            me = here[m]
            h0[m, me] = h1[m].reshape(32, SIDE)
            for d in (1, 3, 2):
                copy = spread_copy(0, m, d, h0.at[m, me], h0.at[m, me])
                copy.start()
                pending.append(copy)
        for m in range(3):
            me = here[m]
            for d in (1, 3, 2):
                slot = h0.at[m, wrap(me - d)]
                spread_copy(0, m, d, slot, slot).wait_recv()
        gf[core] = h0[...].reshape(3, HALF, SIDE)
        join = remote(gf.at[core], gf.at[core], ar_send.at[1], ar_recv.at[1], other_core)
        join.start()
        pending.append(join)
        remote(gf.at[1 - core], gf.at[1 - core], ar_send.at[1], ar_recv.at[1], other_core).wait_recv()
        for m in range(3):
            full[m, :HALF] = gf[0, m]
            full[m, HALF:] = gf[1, m]
        for copy in pending:
            copy.wait_send()

        first = it == 0
        norm[...] = jnp.where(first, full[1], norm[...])
        cross = jnp.where(first, full[0], full[1])
        raw = full[0]
        inv[0] = 0.5 * (raw + raw.T)
        inv[1] = norm[...]
        for m in range(2):
            work[m] = inv[m, :HALF, :HALF]

        def eliminate(half, c_):
            for m, out in enumerate(gauss_jordan([work[0], work[1]], HALF)):
                work[m] = out

            @pl.when(half == 0)
            def _():
                for m in range(2):
                    t = mm(inv[m, HALF:, :HALF], work[m])
                    tri[m] = t
                    corner = inv[m, HALF:, HALF:] - mm(t, inv[m, :HALF, HALF:])
                    inv[m, :HALF, :HALF] = work[m]
                    work[m] = corner

            return c_

        lax.fori_loop(0, 2, eliminate, 0)
        for m in range(2):
            t = tri[m]
            low = mm(work[m], t)
            inv[m, :HALF, :HALF] += mm_t(t, low)
            inv[m, HALF:, :HALF] = -low
            inv[m, :HALF, HALF:] = -low.T
            inv[m, HALF:, HALF:] = work[m]
        alpha = mm(inv[0], norm[...])
        fall = mm(cross, alpha)
        after = norm[...] - fall - fall.T + mm_t(alpha, mm(full[2], alpha))
        beta = mm(inv[1], after)
        norm[...] = after
        small[0] = alpha
        small[1] = beta

        permute_wait(owner_in)
        x_ref[...] += mm(d_ref[...], alpha)
        r_ref[...] -= mm(q[...], alpha)
        d_ref[...] = r_ref[...] + mm(d_ref[...], beta)
        return carry

    lax.fori_loop(0, ITERS, iteration, 0)


def body(covariance, right_side):
    rows, cols = covariance.shape
    piece, side = right_side.shape
    vec = jax.ShapeDtypeStruct((piece, side), F32)
    vmem = pl.BlockSpec(memory_space=pltpu.VMEM)

    def f32(*shape):
        return pltpu.VMEM(shape, F32)

    def dma(n):
        return pltpu.SemaphoreType.DMA((n,))

    return pl.pallas_call(
        kernel,
        out_shape=(vec, vec, vec),
        in_specs=[pl.BlockSpec(memory_space=pl.ANY), vmem],
        out_specs=(vmem, vmem, vmem),
        scratch_shapes=[
            pltpu.VMEM((8, piece, cols), BF16),
            pltpu.VMEM((4, 4, 2, piece // 2, side), BF16),
            f32(8, piece, side),
            pltpu.VMEM((4, piece, side), WIRE),
            pltpu.VMEM((4, piece, side), WIRE),
            pltpu.VMEM((2, piece // 2, side), WIRE),
            pltpu.VMEM((2, piece // 2, side), WIRE),
            pltpu.VMEM((2, piece, side), WIRE),
            pltpu.VMEM((2, piece, side), WIRE),
            f32(piece, side), f32(piece, side), f32(piece, side), f32(piece, side),
            f32(3, side, side), f32(3, HALF, side), f32(3, 4, 32, side), f32(3, 4, 32, side),
            f32(3, 4, 8, side), f32(3, 4, 8, side), f32(3, 8, side), f32(3, 4, 8, side),
            f32(3, 4, 8, side), f32(3, 4, 32, side), f32(2, 3, HALF, side),
            f32(side, side), f32(3, side, side), f32(2, side, side),
            f32(2, HALF, HALF), f32(2, HALF, HALF), f32(2, side, side),
            pltpu.SemaphoreType.DMA,
            dma(40), dma(40), dma(8), dma(8), dma(2), dma(2), dma(56), dma(56),
        ],
        compiler_params=pltpu.CompilerParams(
            collective_id=0, has_side_effects=True, vmem_limit_bytes=60 * 1024 * 1024
        ),
    )(covariance.reshape(8, piece, cols), right_side)


def solution(mesh):
    spec = P(("col", "row"), None)
    return jax.shard_map(
        body,
        mesh=mesh,
        in_specs=(P("row", "col"), spec),
        out_specs=(spec, spec, spec),
        check_vma=False,
    )
```

```python
import functools

import jax
import jax.numpy as jnp
from jax import lax
from jax.experimental import pallas as pl
from jax.experimental.pallas import tpu as pltpu
from jax.sharding import PartitionSpec as P

ITERS = 3
MESH = pl.DeviceIdType.MESH
HIGHEST = lax.Precision.HIGHEST
F32 = jnp.float32
BF16 = jnp.bfloat16
WIRE = jnp.bfloat16
SIDE = 256
HALF = SIDE // 2
RING = 4
OFFS = (0, -1, 1, 2)


def mm(left, right):
    return jnp.dot(left, right, precision=HIGHEST, preferred_element_type=F32)


def mm_t(left, right):
    return lax.dot_general(
        left, right, (((0,), (0,)), ((), ())), precision=HIGHEST, preferred_element_type=F32
    )


def eliminate(mat, size):
    sub = lax.broadcasted_iota(jnp.int32, (8, size), 0)
    lane = lax.broadcasted_iota(jnp.int32, (8, size), 1)
    tiles = [mat[8 * t : 8 * t + 8, :] for t in range(size // 8)]
    for k in range(0, size, 4):
        p, o = k // 8, k % 8
        inside = (lane >= k) & (lane < k + 4)
        col = [[jnp.broadcast_to(v[:, k + j : k + j + 1], (8, size)) for j in range(4)] for v in tiles]
        e = [[col[p][j][o + i : o + i + 1, :] for j in range(4)] for i in range(4)]
        r = [
            jnp.where(lane[:1] == k + j, 1.0, jnp.where(inside[:1], 0.0, tiles[p][o + j : o + j + 1, :]))
            for j in range(4)
        ]
        a0, a1, a2 = e[0][0], e[0][1], e[1][1]
        da = 1.0 / (a0 * a2 - a1 * a1)
        u = [
            [a2 * e[0][2] - a1 * e[1][2], a2 * e[0][3] - a1 * e[1][3]],
            [a0 * e[1][2] - a1 * e[0][2], a0 * e[1][3] - a1 * e[0][3]],
        ]
        s0 = e[2][2] - (e[0][2] * u[0][0] + e[1][2] * u[1][0]) * da
        s1 = e[2][3] - (e[0][2] * u[0][1] + e[1][2] * u[1][1]) * da
        s2 = e[3][3] - (e[0][3] * u[0][1] + e[1][3] * u[1][1]) * da
        t = [[v * da for v in w] for w in u]
        ds = 1.0 / (s0 * s2 - s1 * s1)
        w0 = r[2] - t[0][0] * r[0] - t[1][0] * r[1]
        w1 = r[3] - t[0][1] * r[0] - t[1][1] * r[1]
        q0 = (a2 * r[0] - a1 * r[1]) * da
        q1 = (a0 * r[1] - a1 * r[0]) * da
        b0 = (s2 * w0 - s1 * w1) * ds
        b1 = (s0 * w1 - s1 * w0) * ds
        rows = [q0 - (t[0][0] * b0 + t[0][1] * b1), q1 - (t[1][0] * b0 + t[1][1] * b1), b0, b1]
        rows = [jnp.broadcast_to(v, (8, size)) for v in rows]
        new = []
        for i, v in enumerate(tiles):
            c = col[i]
            if i == p:
                band = (sub >= o) & (sub < o + 4)
                c = [jnp.where(band, jnp.where(sub == o + j, -1.0, 0.0), c[j]) for j in range(4)]
                v = jnp.where(inside | band, 0.0, v)
            else:
                v = jnp.where(inside, 0.0, v)
            new.append((v - c[0] * rows[0] - c[1] * rows[1]) - (c[2] * rows[2] + c[3] * rows[3]))
        tiles = new
    return jnp.concatenate(tiles, axis=0)


def kernel(
    a_hbm, b_ref, x_ref, r_ref, d_ref,
    a, lb, part, t1, s3, t3, rp, dp, qp, q, dold,
    g, gt, g0, u1, g1, u2, g2, u3, h1, h0, gf, norm, full, inv, mat, work, tri, small,
    a_sem, ag_send, ag_recv, rs_send, rs_recv, pm_send, pm_recv, ar_send, ar_recv,
):
    row, col = lax.axis_index("row"), lax.axis_index("col")
    z, y, x, core = row // RING, row % RING, col // 2, col % 2
    here = (x, y, z)

    def wrap(v):
        return (v + 2 * RING) % RING

    def device(pos, c):
        return (pos[2] * RING + pos[1], pos[0] * 2 + c)

    def along(axis, d):
        pos = list(here)
        pos[axis] = wrap(pos[axis] + d)
        return device(pos, core)

    other_core = device(here, 1 - core)

    def remote(src, dst, send, recv, target):
        return pltpu.make_async_remote_copy(
            src_ref=src, dst_ref=dst, send_sem=send, recv_sem=recv, device_id=target, device_id_type=MESH
        )

    load_a = pltpu.make_async_copy(a_hbm, a, a_sem)
    load_a.start()

    piece_out = col * 16 + row
    to_rows = (piece_out // 8, piece_out % 8)
    piece_in = row * 8 + col
    to_owner = (piece_in % 16, piece_in // 16)
    fixed = piece_out == piece_in

    barrier = pltpu.get_barrier_semaphore()

    def greet(target):
        pl.semaphore_signal(barrier, inc=1, device_id=target, device_id_type=MESH)

    for axis in range(3):
        for d in range(1, RING):
            greet(along(axis, d))
    greet(other_core)

    @pl.when(jnp.logical_not(fixed))
    def _():
        greet(to_rows)
        greet(to_owner)

    pl.semaphore_wait(barrier, jnp.where(fixed, 10, 12))

    def permute(src, dst, target, n):
        copy = remote(src, dst, pm_send.at[n], pm_recv.at[n], target)

        @pl.when(jnp.logical_not(fixed))
        def _():
            copy.start()

        @pl.when(fixed)
        def _():
            pltpu.make_async_copy(src, dst, pm_recv.at[n]).start()

        return copy

    def permute_wait(copy):
        copy.wait_recv()

        @pl.when(jnp.logical_not(fixed))
        def _():
            copy.wait_send()

    rows_in = remote(b_ref, rp, pm_send.at[0], pm_recv.at[0], to_rows)

    r_ref[...] = b_ref[...]
    d_ref[...] = b_ref[...]
    x_ref[...] = jnp.zeros_like(x_ref)

    def region(h, c1, c2):
        zc, yc = (c2, c1) if h == 0 else (c1, c2)
        return lb.at[zc, yc, h]

    def gather(h, g_, e, incoming):
        axes = (1, 2) if h == 0 else (2, 1)
        mine = (here[axes[0]], here[axes[1]])
        off = (-1, 1, 2)[e] if incoming else 0
        if g_ == 0:
            c1, c2, axis = wrap(mine[0] + off), mine[1], axes[0]
        else:
            c1, c2, axis = wrap(mine[0] + OFFS[g_ - 1]), wrap(mine[1] + off), axes[1]
        ref = region(h, c1, c2)
        n = h * 15 + g_ * 3 + e
        return remote(ref, ref, ag_send.at[n], ag_recv.at[n], along(axis, (1, -1, 2)[e]))

    def send(h, g_):
        for e in range(3):
            gather(h, g_, e, False).start()

    def take(h, g_, es=(0, 1, 2)):
        for e in es:
            gather(h, g_, e, True).wait_recv()

    def product(zc, j, first):
        cols = pl.ds(pl.multiple_of(zc * 896, 128), 896)
        block = lb[zc].reshape(896, SIDE)
        out = jnp.dot(a[j, :, cols], block, preferred_element_type=F32)
        if first:
            part[j] = out
        else:
            part[j] += out

    def all_products(zc, first):
        def body(j, carry):
            product(zc, j, first)
            return carry

        lax.fori_loop(0, 8, body, 0)

    def shift(i):
        if isinstance(i, int):
            return (2, 1, -1, 0)[i]
        return jnp.where(i == 0, 2, jnp.where(i == 1, 1, jnp.where(i == 2, -1, 0)))

    def core_copy(i):
        j = 2 * wrap(x + shift(i)) + 1 - core
        return remote(part.at[j], t1.at[i], rs_send.at[i], rs_recv.at[i], other_core)

    def ring_copy(i):
        return remote(s3.at[i], t3.at[i], rs_send.at[4 + i], rs_recv.at[4 + i], along(0, shift(i)))

    def reduce_copy(stage, m, d, src, dst):
        axis = (m + stage) % 3
        n = 2 + (stage * 3 + m) * 3 + d - 1
        return remote(src, dst, ar_send.at[n], ar_recv.at[n], along(axis, d))

    def spread_copy(stage, m, d, src, dst):
        axis = (m + stage) % 3
        n = 29 + (stage * 3 + m) * 3 + d - 1
        return remote(src, dst, ar_send.at[n], ar_recv.at[n], along(axis, d))

    def iteration(it, carry):
        lb[z, y] = d_ref[...].astype(BF16).reshape(2, 112, SIDE)
        for h in (0, 1):
            send(h, 0)
            send(h, 1)

        @pl.when(it > 0)
        def _():
            rp[...] = rp[...] - mm(qp[...], small[0])
            dp[...] = rp[...] + mm(dp[...], small[1])

        for k in range(3):
            for h in (0, 1):
                take(h, 0, (k,))
                send(h, k + 2)

        @pl.when(it == 0)
        def _():
            @pl.when(jnp.logical_not(fixed))
            def _():
                rows_in.start()

            @pl.when(fixed)
            def _():
                pltpu.make_async_copy(b_ref, rp, pm_recv.at[0]).start()

            load_a.wait()

        @pl.when(it > 0)
        def _():
            x_ref[...] += mm(dold[...], small[0])

        take(1, 1)
        all_products(z, True)
        for k in (1, 2):
            for g_ in (1, 2, 3, 4):
                take(0, g_, (k - 1,))
            take(1, k + 1)
            all_products(wrap(z + OFFS[k]), False)
        for g_ in (1, 2, 3, 4):
            take(0, g_, (2,))
        take(1, 4)

        last = wrap(z + 2)

        def finish(i, c_):
            j = 2 * wrap(x + shift(i)) + 1 - core
            product(last, j, False)
            core_copy(i).start()
            product(last, 2 * wrap(x + shift(i)) + core, False)
            return c_

        lax.fori_loop(0, 4, finish, 0)

        def chip_sum(i):
            core_copy(i).wait_recv()
            return part[2 * wrap(x + shift(i)) + core] + t1[i]

        for i in range(3):
            s3[i] = chip_sum(i).astype(WIRE)
            ring_copy(i).start()
        own = chip_sum(3)
        for h in (0, 1):
            for g_ in range(5):
                for e in range(3):
                    gather(h, g_, e, False).wait_send()
        for i in range(3):
            ring_copy(i).wait_recv()
        qp[...] = own + (t3[0].astype(F32) + t3[1].astype(F32) + t3[2].astype(F32))

        @pl.when(it == 0)
        def _():
            permute_wait(rows_in)
            dp[...] = rp[...]

        image, res = qp[...], rp[...]
        g[0] = mm_t(dp[...], image)
        g[1] = mm_t(res, jnp.where(it == 0, res, image))
        g[2] = mm_t(image, image)
        theirs = pl.ds(pl.multiple_of((1 - core) * HALF, HALF), HALF)
        ours = pl.ds(pl.multiple_of(core * HALF, HALF), HALF)
        swap = remote(g.at[:, theirs], gt, ar_send.at[0], ar_recv.at[0], other_core)
        swap.start()
        for i in range(4):
            core_copy(i).wait_send()
        for i in range(3):
            ring_copy(i).wait_send()
        swap.wait_recv()
        g0[...] = (g[:, ours] + gt[...]).reshape(3, RING, 32, SIDE)
        pending = [swap]

        def reduce_stage(stage, source, slots, result):
            for m in range(3):
                me = here[(m + stage) % 3]
                for d in (1, 3, 2):
                    src = source.at[m, wrap(me + d)] if stage < 2 else source.at[m]
                    copy = reduce_copy(stage, m, d, src, slots.at[m, me])
                    copy.start()
                    pending.append(copy)
                slots[m, me] = source[m, me] if stage < 2 else source[m]
            for m in range(3):
                me = here[(m + stage) % 3]
                for d in (1, 3, 2):
                    slot = slots.at[m, wrap(me - d)]
                    reduce_copy(stage, m, d, slot, slot).wait_recv()
                result(m, (slots[m, 0] + slots[m, 1]) + (slots[m, 2] + slots[m, 3]))

        def put1(m, v):
            g1[m] = v.reshape(RING, 8, SIDE)

        def put2(m, v):
            g2[m] = v

        def put3(m, v):
            h1[m, here[(m + 1) % 3]] = v

        reduce_stage(0, g0, u1, put1)
        reduce_stage(1, g1, u2, put2)
        reduce_stage(2, g2, u3, put3)
        for m in range(3):
            me = here[(m + 1) % 3]
            for d in (1, 3, 2):
                copy = spread_copy(1, m, d, h1.at[m, me], h1.at[m, me])
                copy.start()
                pending.append(copy)
        for m in range(3):
            me = here[(m + 1) % 3]
            for d in (1, 3, 2):
                slot = h1.at[m, wrap(me - d)]
                spread_copy(1, m, d, slot, slot).wait_recv()
            me = here[m]
            h0[m, me] = h1[m].reshape(32, SIDE)
            for d in (1, 3, 2):
                copy = spread_copy(0, m, d, h0.at[m, me], h0.at[m, me])
                copy.start()
                pending.append(copy)
        for m in range(3):
            me = here[m]
            for d in (1, 3, 2):
                slot = h0.at[m, wrap(me - d)]
                spread_copy(0, m, d, slot, slot).wait_recv()
        gf[core] = h0[...].reshape(3, HALF, SIDE)
        join = remote(gf.at[core], gf.at[core], ar_send.at[1], ar_recv.at[1], other_core)
        join.start()
        pending.append(join)
        remote(gf.at[1 - core], gf.at[1 - core], ar_send.at[1], ar_recv.at[1], other_core).wait_recv()
        for m in range(3):
            full[m, :HALF] = gf[0, m]
            full[m, HALF:] = gf[1, m]
        for copy in pending:
            copy.wait_send()

        owner_in = permute(qp, q, to_owner, 1)

        first = it == 0
        norm[...] = jnp.where(first, full[1], norm[...])
        cross = jnp.where(first, full[0], full[1])
        raw = full[0]
        mat[...] = jnp.where(core == 0, 0.5 * (raw + raw.T), norm[...])
        work[...] = mat[:HALF, :HALF]

        def half_step(half, c_):
            work[...] = eliminate(work[...], HALF)

            @pl.when(half == 0)
            def _():
                t = mm(mat[HALF:, :HALF], work[...])
                tri[...] = t
                corner = mat[HALF:, HALF:] - mm(t, mat[:HALF, HALF:])
                mat[:HALF, :HALF] = work[...]
                work[...] = corner

            return c_

        lax.fori_loop(0, 2, half_step, 0)
        t = tri[...]
        low = mm(work[...], t)
        inv[core, :HALF, :HALF] = mat[:HALF, :HALF] + mm_t(t, low)
        inv[core, HALF:, :HALF] = -low
        inv[core, :HALF, HALF:] = -low.T
        inv[core, HALF:, HALF:] = work[...]
        share = remote(inv.at[core], inv.at[core], ar_send.at[56], ar_recv.at[56], other_core)
        share.start()
        remote(inv.at[1 - core], inv.at[1 - core], ar_send.at[56], ar_recv.at[56], other_core).wait_recv()
        alpha = mm(inv[0], norm[...])
        fall = mm(cross, alpha)
        after = norm[...] - fall - fall.T + mm_t(alpha, mm(full[2], alpha))
        beta = mm(inv[1], after)
        norm[...] = after
        small[0] = alpha
        small[1] = beta

        permute_wait(owner_in)
        r_ref[...] -= mm(q[...], alpha)
        dold[...] = d_ref[...]
        d_ref[...] = r_ref[...] + mm(d_ref[...], beta)
        share.wait_send()
        return carry

    lax.fori_loop(0, ITERS, iteration, 0)
    x_ref[...] += mm(dold[...], small[0])


def body(covariance, right_side):
    rows, cols = covariance.shape
    piece, side = right_side.shape
    vec = jax.ShapeDtypeStruct((piece, side), F32)
    vmem = pl.BlockSpec(memory_space=pltpu.VMEM)

    def f32(*shape):
        return pltpu.VMEM(shape, F32)

    def dma(n):
        return pltpu.SemaphoreType.DMA((n,))

    return pl.pallas_call(
        kernel,
        out_shape=(vec, vec, vec),
        in_specs=[pl.BlockSpec(memory_space=pl.ANY), vmem],
        out_specs=(vmem, vmem, vmem),
        scratch_shapes=[
            pltpu.VMEM((8, piece, cols), BF16),
            pltpu.VMEM((4, 4, 2, piece // 2, side), BF16),
            f32(8, piece, side),
            f32(4, piece, side),
            pltpu.VMEM((3, piece, side), WIRE),
            pltpu.VMEM((3, piece, side), WIRE),
            f32(piece, side), f32(piece, side), f32(piece, side), f32(piece, side), f32(piece, side),
            f32(3, side, side), f32(3, HALF, side), f32(3, 4, 32, side), f32(3, 4, 32, side),
            f32(3, 4, 8, side), f32(3, 4, 8, side), f32(3, 8, side), f32(3, 4, 8, side),
            f32(3, 4, 8, side), f32(3, 4, 32, side), f32(2, 3, HALF, side),
            f32(side, side), f32(3, side, side), f32(2, side, side),
            f32(side, side), f32(HALF, HALF), f32(HALF, HALF), f32(2, side, side),
            pltpu.SemaphoreType.DMA,
            dma(30), dma(30), dma(7), dma(7), dma(2), dma(2), dma(57), dma(57),
        ],
        compiler_params=pltpu.CompilerParams(
            collective_id=0, has_side_effects=True, vmem_limit_bytes=60 * 1024 * 1024
        ),
    )(covariance.reshape(8, piece, cols), right_side)


def solution(mesh):
    spec = P(("col", "row"), None)
    return jax.shard_map(
        body,
        mesh=mesh,
        in_specs=(P("row", "col"), spec),
        out_specs=(spec, spec, spec),
        check_vma=False,
    )
```

```python
import functools

import jax
import jax.numpy as jnp
from jax import lax
from jax.experimental import pallas as pl
from jax.experimental.pallas import tpu as pltpu
from jax.sharding import PartitionSpec as P

ITERS = 3
MESH = pl.DeviceIdType.MESH
HIGHEST = lax.Precision.HIGHEST
F32 = jnp.float32
BF16 = jnp.bfloat16
WIRE = jnp.bfloat16
SIDE = 256
HALF = SIDE // 2
RING = 4
OFFS = (0, -1, 1, 2)


def mm(left, right):
    return jnp.dot(left, right, precision=HIGHEST, preferred_element_type=F32)


def mm_t(left, right):
    return lax.dot_general(
        left, right, (((0,), (0,)), ((), ())), precision=HIGHEST, preferred_element_type=F32
    )


def eliminate(mat, size):
    sub = lax.broadcasted_iota(jnp.int32, (8, size), 0)
    lane = lax.broadcasted_iota(jnp.int32, (8, size), 1)
    tiles = [mat[8 * t : 8 * t + 8, :] for t in range(size // 8)]
    for k in range(0, size, 4):
        p, o = k // 8, k % 8
        inside = (lane >= k) & (lane < k + 4)
        col = [[jnp.broadcast_to(v[:, k + j : k + j + 1], (8, size)) for j in range(4)] for v in tiles]
        e = [[col[p][j][o + i : o + i + 1, :] for j in range(4)] for i in range(4)]
        r = [
            jnp.where(lane[:1] == k + j, 1.0, jnp.where(inside[:1], 0.0, tiles[p][o + j : o + j + 1, :]))
            for j in range(4)
        ]
        a0, a1, a2 = e[0][0], e[0][1], e[1][1]
        da = 1.0 / (a0 * a2 - a1 * a1)
        u = [
            [a2 * e[0][2] - a1 * e[1][2], a2 * e[0][3] - a1 * e[1][3]],
            [a0 * e[1][2] - a1 * e[0][2], a0 * e[1][3] - a1 * e[0][3]],
        ]
        s0 = e[2][2] - (e[0][2] * u[0][0] + e[1][2] * u[1][0]) * da
        s1 = e[2][3] - (e[0][2] * u[0][1] + e[1][2] * u[1][1]) * da
        s2 = e[3][3] - (e[0][3] * u[0][1] + e[1][3] * u[1][1]) * da
        t = [[v * da for v in w] for w in u]
        ds = 1.0 / (s0 * s2 - s1 * s1)
        w0 = r[2] - t[0][0] * r[0] - t[1][0] * r[1]
        w1 = r[3] - t[0][1] * r[0] - t[1][1] * r[1]
        q0 = (a2 * r[0] - a1 * r[1]) * da
        q1 = (a0 * r[1] - a1 * r[0]) * da
        b0 = (s2 * w0 - s1 * w1) * ds
        b1 = (s0 * w1 - s1 * w0) * ds
        rows = [q0 - (t[0][0] * b0 + t[0][1] * b1), q1 - (t[1][0] * b0 + t[1][1] * b1), b0, b1]
        rows = [jnp.broadcast_to(v, (8, size)) for v in rows]
        new = []
        for i, v in enumerate(tiles):
            c = col[i]
            if i == p:
                band = (sub >= o) & (sub < o + 4)
                c = [jnp.where(band, jnp.where(sub == o + j, -1.0, 0.0), c[j]) for j in range(4)]
                v = jnp.where(inside | band, 0.0, v)
            else:
                v = jnp.where(inside, 0.0, v)
            new.append((v - c[0] * rows[0] - c[1] * rows[1]) - (c[2] * rows[2] + c[3] * rows[3]))
        tiles = new
    return jnp.concatenate(tiles, axis=0)


def kernel(
    a_hbm, b_ref, x_ref, r_ref, d_ref,
    a, lb, part, t1, s3, t3, rp, dp, qp, q, dold,
    g, gt, g0, u1, g2, u3, h0, gf, norm, full, inv, mat, work, tri, small,
    a_sem, ag_send, ag_recv, rs_send, rs_recv, pm_send, pm_recv, ar_send, ar_recv,
):
    row, col = lax.axis_index("row"), lax.axis_index("col")
    z, y, x, core = row // RING, row % RING, col // 2, col % 2
    here = (x, y, z)

    def wrap(v):
        return (v + 2 * RING) % RING

    def device(pos, c):
        return (pos[2] * RING + pos[1], pos[0] * 2 + c)

    def along(axis, d):
        pos = list(here)
        pos[axis] = wrap(pos[axis] + d)
        return device(pos, core)

    other_core = device(here, 1 - core)

    def in_plane(m, d, f):
        pos = list(here)
        pos[m] = wrap(pos[m] + d)
        pos[(m + 1) % 3] = wrap(pos[(m + 1) % 3] + f)
        return device(pos, core)

    def remote(src, dst, send, recv, target):
        return pltpu.make_async_remote_copy(
            src_ref=src, dst_ref=dst, send_sem=send, recv_sem=recv, device_id=target, device_id_type=MESH
        )

    load_a = pltpu.make_async_copy(a_hbm, a, a_sem)
    load_a.start()

    piece_out = col * 16 + row
    to_rows = (piece_out // 8, piece_out % 8)
    piece_in = row * 8 + col
    to_owner = (piece_in % 16, piece_in // 16)
    fixed = piece_out == piece_in

    barrier = pltpu.get_barrier_semaphore()

    def greet(target):
        pl.semaphore_signal(barrier, inc=1, device_id=target, device_id_type=MESH)

    for axis in range(3):
        for d in range(1, RING):
            greet(along(axis, d))
    greet(other_core)
    for m in range(3):
        for d in range(1, RING):
            for f in range(1, RING):
                greet(in_plane(m, d, f))

    @pl.when(jnp.logical_not(fixed))
    def _():
        greet(to_rows)
        greet(to_owner)

    pl.semaphore_wait(barrier, jnp.where(fixed, 37, 39))

    def permute(src, dst, target, n):
        copy = remote(src, dst, pm_send.at[n], pm_recv.at[n], target)

        @pl.when(jnp.logical_not(fixed))
        def _():
            copy.start()

        @pl.when(fixed)
        def _():
            pltpu.make_async_copy(src, dst, pm_recv.at[n]).start()

        return copy

    def permute_wait(copy):
        copy.wait_recv()

        @pl.when(jnp.logical_not(fixed))
        def _():
            copy.wait_send()

    rows_in = remote(b_ref, rp, pm_send.at[0], pm_recv.at[0], to_rows)

    r_ref[...] = b_ref[...]
    d_ref[...] = b_ref[...]
    x_ref[...] = jnp.zeros_like(x_ref)

    def region(h, c1, c2):
        zc, yc = (c2, c1) if h == 0 else (c1, c2)
        return lb.at[zc, yc, h]

    def gather(h, g_, e, incoming):
        axes = (1, 2) if h == 0 else (2, 1)
        mine = (here[axes[0]], here[axes[1]])
        off = (-1, 1, 2)[e] if incoming else 0
        if g_ == 0:
            c1, c2, axis = wrap(mine[0] + off), mine[1], axes[0]
        else:
            c1, c2, axis = wrap(mine[0] + OFFS[g_ - 1]), wrap(mine[1] + off), axes[1]
        ref = region(h, c1, c2)
        n = h * 15 + g_ * 3 + e
        return remote(ref, ref, ag_send.at[n], ag_recv.at[n], along(axis, (1, -1, 2)[e]))

    def send(h, g_):
        for e in range(3):
            gather(h, g_, e, False).start()

    def take(h, g_, es=(0, 1, 2)):
        for e in es:
            gather(h, g_, e, True).wait_recv()

    def product(zc, j, first):
        cols = pl.ds(pl.multiple_of(zc * 896, 128), 896)
        block = lb[zc].reshape(896, SIDE)
        out = jnp.dot(a[j, :, cols], block, preferred_element_type=F32)
        if first:
            part[j] = out
        else:
            part[j] += out

    def all_products(zc, first):
        def body(j, carry):
            product(zc, j, first)
            return carry

        lax.fori_loop(0, 8, body, 0)

    def shift(i):
        if isinstance(i, int):
            return (2, 1, -1, 0)[i]
        return jnp.where(i == 0, 2, jnp.where(i == 1, 1, jnp.where(i == 2, -1, 0)))

    def core_copy(i):
        j = 2 * wrap(x + shift(i)) + 1 - core
        return remote(part.at[j], t1.at[i], rs_send.at[i], rs_recv.at[i], other_core)

    def ring_copy(i):
        return remote(s3.at[i], t3.at[i], rs_send.at[4 + i], rs_recv.at[4 + i], along(0, shift(i)))

    def plane_copy(base, m, k, src, dst):
        n = base + 16 * m + k
        return remote(src, dst, ar_send.at[n], ar_recv.at[n], in_plane(m, k // 4, k % 4))

    def line_copy(m, d, src, dst):
        n = 96 + 3 * m + d - 1
        return remote(src, dst, ar_send.at[n], ar_recv.at[n], along((m + 2) % 3, d))

    def iteration(it, carry):
        lb[z, y] = d_ref[...].astype(BF16).reshape(2, 112, SIDE)
        for g_ in (0, 1):
            for h in (0, 1):
                send(h, g_)

        @pl.when(it > 0)
        def _():
            rp[...] = rp[...] - mm(qp[...], small[0])
            dp[...] = rp[...] + mm(dp[...], small[1])

        for k in range(3):
            for h in (0, 1):
                take(h, 0, (k,))
                send(h, k + 2)

        @pl.when(it == 0)
        def _():
            @pl.when(jnp.logical_not(fixed))
            def _():
                rows_in.start()

            @pl.when(fixed)
            def _():
                pltpu.make_async_copy(b_ref, rp, pm_recv.at[0]).start()

            load_a.wait()

        @pl.when(it > 0)
        def _():
            x_ref[...] += mm(dold[...], small[0])

        take(1, 1)
        all_products(z, True)
        for k in (1, 2):
            for g_ in (1, 2, 3, 4):
                take(0, g_, (k - 1,))
            take(1, k + 1)
            all_products(wrap(z + OFFS[k]), False)
        for g_ in (1, 2, 3, 4):
            take(0, g_, (2,))
        take(1, 4)

        last = wrap(z + 2)

        def finish(i, c_):
            j = 2 * wrap(x + shift(i)) + 1 - core
            product(last, j, False)
            core_copy(i).start()
            product(last, 2 * wrap(x + shift(i)) + core, False)
            return c_

        lax.fori_loop(0, 4, finish, 0)

        def chip_sum(i):
            core_copy(i).wait_recv()
            return part[2 * wrap(x + shift(i)) + core] + t1[i]

        for i in range(3):
            s3[i] = chip_sum(i).astype(WIRE)
            ring_copy(i).start()
        own = chip_sum(3)
        for h in (0, 1):
            for g_ in range(5):
                for e in range(3):
                    gather(h, g_, e, False).wait_send()
        for i in range(3):
            ring_copy(i).wait_recv()
        qp[...] = own + (t3[0].astype(F32) + t3[1].astype(F32) + t3[2].astype(F32))

        @pl.when(it == 0)
        def _():
            permute_wait(rows_in)
            dp[...] = rp[...]

        image, res = qp[...], rp[...]
        g[0] = mm_t(dp[...], image)
        g[1] = mm_t(res, jnp.where(it == 0, res, image))
        g[2] = mm_t(image, image)
        theirs = pl.ds(pl.multiple_of((1 - core) * HALF, HALF), HALF)
        ours = pl.ds(pl.multiple_of(core * HALF, HALF), HALF)
        swap = remote(g.at[:, theirs], gt, ar_send.at[105], ar_recv.at[105], other_core)
        swap.start()
        for i in range(4):
            core_copy(i).wait_send()
        for i in range(3):
            ring_copy(i).wait_send()
        swap.wait_recv()
        g0[...] = (g[:, ours] + gt[...]).reshape(3, RING, RING, 8, SIDE)
        pending = [swap]

        def each(m, fn):
            i, j = here[m], here[(m + 1) % 3]

            def step(k, c_):
                fn(k, i, j)
                return c_

            lax.fori_loop(1, 16, step, 0)

        def reduce_send(m, k, i, j):
            src = g0.at[m, wrap(i + k // 4), wrap(j + k % 4)]
            return plane_copy(0, m, k, src, u1.at[m, i, j])

        def spread_send(m, k, i, j):
            return plane_copy(48, m, k, h0.at[m, i, j], h0.at[m, i, j])

        for m in range(3):
            each(m, lambda k, i, j: reduce_send(m, k, i, j).start())
            i, j = here[m], here[(m + 1) % 3]
            u1[m, i, j] = g0[m, i, j]
        for m in range(3):
            def arrived(k, i, j):
                slot = u1.at[m, wrap(i - k // 4), wrap(j - k % 4)]
                plane_copy(0, m, k, slot, slot).wait_recv()

            each(m, arrived)
            g2[m] = jnp.sum(u1[m].reshape(16, 8, SIDE), axis=0)
            me = here[(m + 2) % 3]
            for d in (1, 3, 2):
                copy = line_copy(m, d, g2.at[m], u3.at[m, me])
                copy.start()
                pending.append(copy)
            u3[m, me] = g2[m]
        for m in range(3):
            me = here[(m + 2) % 3]
            for d in (1, 3, 2):
                slot = u3.at[m, wrap(me - d)]
                line_copy(m, d, slot, slot).wait_recv()
            h0[m, here[m], here[(m + 1) % 3]] = (u3[m, 0] + u3[m, 1]) + (u3[m, 2] + u3[m, 3])
            each(m, lambda k, i, j: spread_send(m, k, i, j).start())
        for m in range(3):
            def landed(k, i, j):
                slot = h0.at[m, wrap(i - k // 4), wrap(j - k % 4)]
                plane_copy(48, m, k, slot, slot).wait_recv()

            each(m, landed)
        gf[core] = h0[...].reshape(3, HALF, SIDE)
        join = remote(gf.at[core], gf.at[core], ar_send.at[106], ar_recv.at[106], other_core)
        join.start()
        pending.append(join)
        remote(gf.at[1 - core], gf.at[1 - core], ar_send.at[106], ar_recv.at[106], other_core).wait_recv()
        for m in range(3):
            full[m, :HALF] = gf[0, m]
            full[m, HALF:] = gf[1, m]
        for copy in pending:
            copy.wait_send()
        for m in range(3):
            each(m, lambda k, i, j: reduce_send(m, k, i, j).wait_send())
            each(m, lambda k, i, j: spread_send(m, k, i, j).wait_send())

        owner_in = permute(qp, q, to_owner, 1)

        first = it == 0
        norm[...] = jnp.where(first, full[1], norm[...])
        cross = jnp.where(first, full[0], full[1])
        raw = full[0]
        mat[...] = jnp.where(core == 0, 0.5 * (raw + raw.T), norm[...])
        work[...] = mat[:HALF, :HALF]

        def half_step(half, c_):
            work[...] = eliminate(work[...], HALF)

            @pl.when(half == 0)
            def _():
                t = mm(mat[HALF:, :HALF], work[...])
                tri[...] = t
                corner = mat[HALF:, HALF:] - mm(t, mat[:HALF, HALF:])
                mat[:HALF, :HALF] = work[...]
                work[...] = corner

            return c_

        lax.fori_loop(0, 2, half_step, 0)
        t = tri[...]
        low = mm(work[...], t)
        inv[core, :HALF, :HALF] = mat[:HALF, :HALF] + mm_t(t, low)
        inv[core, HALF:, :HALF] = -low
        inv[core, :HALF, HALF:] = -low.T
        inv[core, HALF:, HALF:] = work[...]
        share = remote(inv.at[core], inv.at[core], ar_send.at[107], ar_recv.at[107], other_core)
        share.start()
        remote(inv.at[1 - core], inv.at[1 - core], ar_send.at[107], ar_recv.at[107], other_core).wait_recv()
        alpha = mm(inv[0], norm[...])
        fall = mm(cross, alpha)
        after = norm[...] - fall - fall.T + mm_t(alpha, mm(full[2], alpha))
        beta = mm(inv[1], after)
        norm[...] = after
        small[0] = alpha
        small[1] = beta

        permute_wait(owner_in)
        r_ref[...] -= mm(q[...], alpha)
        dold[...] = d_ref[...]
        d_ref[...] = r_ref[...] + mm(d_ref[...], beta)
        share.wait_send()
        return carry

    lax.fori_loop(0, ITERS, iteration, 0)
    x_ref[...] += mm(dold[...], small[0])


def body(covariance, right_side):
    rows, cols = covariance.shape
    piece, side = right_side.shape
    vec = jax.ShapeDtypeStruct((piece, side), F32)
    vmem = pl.BlockSpec(memory_space=pltpu.VMEM)

    def f32(*shape):
        return pltpu.VMEM(shape, F32)

    def dma(n):
        return pltpu.SemaphoreType.DMA((n,))

    out = pl.pallas_call(
        kernel,
        out_shape=(vec, vec, vec),
        in_specs=[pl.BlockSpec(memory_space=pl.ANY), vmem],
        out_specs=(vmem, vmem, vmem),
        scratch_shapes=[
            pltpu.VMEM((8, piece, cols), BF16),
            pltpu.VMEM((4, 4, 2, piece // 2, side), BF16),
            f32(8, piece, side),
            f32(4, piece, side),
            pltpu.VMEM((3, piece, side), WIRE),
            pltpu.VMEM((3, piece, side), WIRE),
            f32(piece, side), f32(piece, side), f32(piece, side), f32(piece, side), f32(piece, side),
            f32(3, side, side), f32(3, HALF, side), f32(3, 4, 4, 8, side), f32(3, 4, 4, 8, side),
            f32(3, 8, side), f32(3, 4, 8, side), f32(3, 4, 4, 8, side), f32(2, 3, HALF, side),
            f32(side, side), f32(3, side, side), f32(2, side, side),
            f32(side, side), f32(HALF, HALF), f32(HALF, HALF), f32(2, side, side),
            pltpu.SemaphoreType.DMA,
            dma(30), dma(30), dma(7), dma(7), dma(2), dma(2), dma(108), dma(108),
        ],
        compiler_params=pltpu.CompilerParams(
            collective_id=0, has_side_effects=True, vmem_limit_bytes=60 * 1024 * 1024
        ),
    )(covariance.reshape(8, piece, cols), right_side)

    def hand_over(*refs):
        for src, dst in zip(refs[:3], refs[3:]):
            dst[...] = src[...]

    return pl.pallas_call(hand_over, out_shape=(vec, vec, vec))(*out)


def solution(mesh):
    spec = P(("col", "row"), None)
    return jax.shard_map(
        body,
        mesh=mesh,
        in_specs=(P("row", "col"), spec),
        out_specs=(spec, spec, spec),
        check_vma=False,
    )
```

```python
import functools

import jax
import jax.numpy as jnp
from jax import lax
from jax.experimental import pallas as pl
from jax.experimental.pallas import tpu as pltpu
from jax.sharding import PartitionSpec as P

ITERS = 3
MESH = pl.DeviceIdType.MESH
HIGHEST = lax.Precision.HIGHEST
F32 = jnp.float32
BF16 = jnp.bfloat16
WIRE = jnp.bfloat16
SIDE = 256
HALF = SIDE // 2
RING = 4
OFFS = (0, -1, 1, 2)


def mm(left, right):
    return jnp.dot(left, right, precision=HIGHEST, preferred_element_type=F32)


def mm_t(left, right):
    return lax.dot_general(
        left, right, (((0,), (0,)), ((), ())), precision=HIGHEST, preferred_element_type=F32
    )


def eliminate(mat, size):
    sub = lax.broadcasted_iota(jnp.int32, (8, size), 0)
    lane = lax.broadcasted_iota(jnp.int32, (8, size), 1)
    tiles = [mat[8 * t : 8 * t + 8, :] for t in range(size // 8)]
    lower, scaled = [], []
    for k in range(0, size, 4):
        p, o = k // 8, k % 8
        inside = (lane >= k) & (lane < k + 4)
        live = range(p if o == 0 else p + 1, size // 8)
        col = {
            i: [jnp.broadcast_to(tiles[i][:, k + j : k + j + 1], (8, size)) for j in range(4)]
            for i in sorted({p, *live})
        }
        e = [[col[p][j][o + i : o + i + 1, :] for j in range(4)] for i in range(4)]
        pivot = jnp.where(inside, jnp.where(lane - k == sub - o, 1.0, 0.0), tiles[p])
        r = [pivot[o + j : o + j + 1, :] for j in range(4)]
        a0, a1, a2 = e[0][0], e[0][1], e[1][1]
        da = 1.0 / (a0 * a2 - a1 * a1)
        u = [
            [a2 * e[0][2] - a1 * e[1][2], a2 * e[0][3] - a1 * e[1][3]],
            [a0 * e[1][2] - a1 * e[0][2], a0 * e[1][3] - a1 * e[0][3]],
        ]
        s0 = e[2][2] - (e[0][2] * u[0][0] + e[1][2] * u[1][0]) * da
        s1 = e[2][3] - (e[0][2] * u[0][1] + e[1][2] * u[1][1]) * da
        s2 = e[3][3] - (e[0][3] * u[0][1] + e[1][3] * u[1][1]) * da
        t = [[v * da for v in w] for w in u]
        ds = 1.0 / (s0 * s2 - s1 * s1)
        w0 = r[2] - t[0][0] * r[0] - t[1][0] * r[1]
        w1 = r[3] - t[0][1] * r[0] - t[1][1] * r[1]
        q0 = (a2 * r[0] - a1 * r[1]) * da
        q1 = (a0 * r[1] - a1 * r[0]) * da
        b0 = (s2 * w0 - s1 * w1) * ds
        b1 = (s0 * w1 - s1 * w0) * ds
        rows = [q0 - (t[0][0] * b0 + t[0][1] * b1), q1 - (t[1][0] * b0 + t[1][1] * b1), b0, b1]
        rows = [jnp.broadcast_to(v, (8, size)) for v in rows]
        left = lane < k + 4
        piece = jnp.where(sub == o, rows[0], jnp.where(sub == o + 1, rows[1], jnp.where(sub == o + 2, rows[2], rows[3])))
        pivot, piece = jnp.where(left, pivot, 0.0), jnp.where(left, piece, 0.0)
        if o == 0:
            lower.append(pivot)
            scaled.append(piece)
        else:
            lower[p] = jnp.where(sub < 4, lower[p], pivot)
            scaled[p] = jnp.where(sub < 4, scaled[p], piece)
        for i in live:
            c, v = col[i], jnp.where(inside, 0.0, tiles[i])
            tiles[i] = (v - c[0] * rows[0] - c[1] * rows[1]) - (c[2] * rows[2] + c[3] * rows[3])
    return mm_t(jnp.concatenate(lower, axis=0), jnp.concatenate(scaled, axis=0))


def kernel(
    a_hbm, b_ref, x_ref, r_ref, d_ref,
    a, lb, part, t1, s3, t3, rp, dp, qp, q, dold,
    g, gt, g0, u1, g2, u3, h0, gf, norm, full, inv, mat, work, tri, small,
    a_sem, ag_send, ag_recv, rs_send, rs_recv, pm_send, pm_recv, ar_send, ar_recv,
):
    row, col = lax.axis_index("row"), lax.axis_index("col")
    z, y, x, core = row // RING, row % RING, col // 2, col % 2
    here = (x, y, z)

    def wrap(v):
        return (v + 2 * RING) % RING

    def device(pos, c):
        return (pos[2] * RING + pos[1], pos[0] * 2 + c)

    def along(axis, d):
        pos = list(here)
        pos[axis] = wrap(pos[axis] + d)
        return device(pos, core)

    other_core = device(here, 1 - core)

    def in_plane(m, d, f):
        pos = list(here)
        pos[m] = wrap(pos[m] + d)
        pos[(m + 1) % 3] = wrap(pos[(m + 1) % 3] + f)
        return device(pos, core)

    def remote(src, dst, send, recv, target):
        return pltpu.make_async_remote_copy(
            src_ref=src, dst_ref=dst, send_sem=send, recv_sem=recv, device_id=target, device_id_type=MESH
        )

    load_a = pltpu.make_async_copy(a_hbm, a, a_sem)
    load_a.start()

    piece_out = col * 16 + row
    to_rows = (piece_out // 8, piece_out % 8)
    piece_in = row * 8 + col
    to_owner = (piece_in % 16, piece_in // 16)
    fixed = piece_out == piece_in

    barrier = pltpu.get_barrier_semaphore()

    def greet(target):
        pl.semaphore_signal(barrier, inc=1, device_id=target, device_id_type=MESH)

    for axis in range(3):
        for d in range(1, RING):
            greet(along(axis, d))
    greet(other_core)
    for m in range(3):
        for d in range(1, RING):
            for f in range(1, RING):
                greet(in_plane(m, d, f))

    @pl.when(jnp.logical_not(fixed))
    def _():
        greet(to_rows)
        greet(to_owner)

    pl.semaphore_wait(barrier, jnp.where(fixed, 37, 39))

    def permute(src, dst, target, n):
        copy = remote(src, dst, pm_send.at[n], pm_recv.at[n], target)

        @pl.when(jnp.logical_not(fixed))
        def _():
            copy.start()

        @pl.when(fixed)
        def _():
            pltpu.make_async_copy(src, dst, pm_recv.at[n]).start()

        return copy

    def permute_wait(copy):
        copy.wait_recv()

        @pl.when(jnp.logical_not(fixed))
        def _():
            copy.wait_send()

    rows_in = remote(b_ref, rp, pm_send.at[0], pm_recv.at[0], to_rows)

    r_ref[...] = b_ref[...]
    d_ref[...] = b_ref[...]
    x_ref[...] = jnp.zeros_like(x_ref)

    def region(h, c1, c2):
        zc, yc = (c2, c1) if h == 0 else (c1, c2)
        return lb.at[zc, yc, h]

    def gather(h, g_, e, incoming):
        axes = (1, 2) if h == 0 else (2, 1)
        mine = (here[axes[0]], here[axes[1]])
        off = (-1, 1, 2)[e] if incoming else 0
        if g_ == 0:
            c1, c2, axis = wrap(mine[0] + off), mine[1], axes[0]
        else:
            c1, c2, axis = wrap(mine[0] + OFFS[g_ - 1]), wrap(mine[1] + off), axes[1]
        ref = region(h, c1, c2)
        n = h * 15 + g_ * 3 + e
        return remote(ref, ref, ag_send.at[n], ag_recv.at[n], along(axis, (1, -1, 2)[e]))

    def send(h, g_):
        for e in range(3):
            gather(h, g_, e, False).start()

    def take(h, g_, es=(0, 1, 2)):
        for e in es:
            gather(h, g_, e, True).wait_recv()

    def product(zc, j, first):
        cols = pl.ds(pl.multiple_of(zc * 896, 128), 896)
        block = lb[zc].reshape(896, SIDE)
        out = jnp.dot(a[j, :, cols], block, preferred_element_type=F32)
        if first:
            part[j] = out
        else:
            part[j] += out

    def all_products(zc, first):
        def body(j, carry):
            product(zc, j, first)
            return carry

        lax.fori_loop(0, 8, body, 0)

    def shift(i):
        if isinstance(i, int):
            return (2, 1, -1, 0)[i]
        return jnp.where(i == 0, 2, jnp.where(i == 1, 1, jnp.where(i == 2, -1, 0)))

    def core_copy(i):
        j = 2 * wrap(x + shift(i)) + 1 - core
        return remote(part.at[j], t1.at[i], rs_send.at[i], rs_recv.at[i], other_core)

    def ring_copy(i):
        return remote(s3.at[i], t3.at[i], rs_send.at[4 + i], rs_recv.at[4 + i], along(0, shift(i)))

    def plane_copy(base, m, k, src, dst):
        n = base + 16 * m + k
        return remote(src, dst, ar_send.at[n], ar_recv.at[n], in_plane(m, k // 4, k % 4))

    def line_copy(m, d, src, dst):
        n = 96 + 3 * m + d - 1
        return remote(src, dst, ar_send.at[n], ar_recv.at[n], along((m + 2) % 3, d))

    def iteration(it, carry):
        lb[z, y] = d_ref[...].astype(BF16).reshape(2, 112, SIDE)
        for g_ in (0, 1):
            for h in (0, 1):
                send(h, g_)

        @pl.when(it > 0)
        def _():
            rp[...] = rp[...] - mm(qp[...], small[0])
            dp[...] = rp[...] + mm(dp[...], small[1])

        for k in range(3):
            for h in (0, 1):
                take(h, 0, (k,))
                send(h, k + 2)

        @pl.when(it == 0)
        def _():
            @pl.when(jnp.logical_not(fixed))
            def _():
                rows_in.start()

            @pl.when(fixed)
            def _():
                pltpu.make_async_copy(b_ref, rp, pm_recv.at[0]).start()

            load_a.wait()

        @pl.when(it > 0)
        def _():
            x_ref[...] += mm(dold[...], small[0])

        take(1, 1)
        all_products(z, True)
        for k in (1, 2):
            for g_ in (1, 2, 3, 4):
                take(0, g_, (k - 1,))
            take(1, k + 1)
            all_products(wrap(z + OFFS[k]), False)
        for g_ in (1, 2, 3, 4):
            take(0, g_, (2,))
        take(1, 4)

        last = wrap(z + 2)

        def finish(i, c_):
            j = 2 * wrap(x + shift(i)) + 1 - core
            product(last, j, False)
            core_copy(i).start()
            product(last, 2 * wrap(x + shift(i)) + core, False)
            return c_

        lax.fori_loop(0, 4, finish, 0)

        def chip_sum(i):
            core_copy(i).wait_recv()
            return part[2 * wrap(x + shift(i)) + core] + t1[i]

        for i in range(3):
            s3[i] = chip_sum(i).astype(WIRE)
            ring_copy(i).start()
        own = chip_sum(3)
        for h in (0, 1):
            for g_ in range(5):
                for e in range(3):
                    gather(h, g_, e, False).wait_send()
        for i in range(3):
            ring_copy(i).wait_recv()
        qp[...] = own + (t3[0].astype(F32) + t3[1].astype(F32) + t3[2].astype(F32))

        @pl.when(it == 0)
        def _():
            permute_wait(rows_in)
            dp[...] = rp[...]

        image, res = qp[...], rp[...]
        g[0] = mm_t(dp[...], image)
        g[1] = mm_t(res, jnp.where(it == 0, res, image))
        g[2] = mm_t(image, image)
        theirs = pl.ds(pl.multiple_of((1 - core) * HALF, HALF), HALF)
        ours = pl.ds(pl.multiple_of(core * HALF, HALF), HALF)
        swap = remote(g.at[:, theirs], gt, ar_send.at[105], ar_recv.at[105], other_core)
        swap.start()
        for i in range(4):
            core_copy(i).wait_send()
        for i in range(3):
            ring_copy(i).wait_send()
        swap.wait_recv()
        g0[...] = (g[:, ours] + gt[...]).reshape(3, RING, RING, 8, SIDE)
        pending = [swap]

        def each(m, fn):
            i, j = here[m], here[(m + 1) % 3]

            def step(k, c_):
                fn(k, i, j)
                return c_

            lax.fori_loop(1, 16, step, 0)

        def reduce_send(m, k, i, j):
            src = g0.at[m, wrap(i + k // 4), wrap(j + k % 4)]
            return plane_copy(0, m, k, src, u1.at[m, i, j])

        def spread_send(m, k, i, j):
            return plane_copy(48, m, k, h0.at[m, i, j], h0.at[m, i, j])

        for m in range(3):
            each(m, lambda k, i, j: reduce_send(m, k, i, j).start())
            i, j = here[m], here[(m + 1) % 3]
            u1[m, i, j] = g0[m, i, j]
        for m in range(3):
            def arrived(k, i, j):
                slot = u1.at[m, wrap(i - k // 4), wrap(j - k % 4)]
                plane_copy(0, m, k, slot, slot).wait_recv()

            each(m, arrived)
            g2[m] = jnp.sum(u1[m].reshape(16, 8, SIDE), axis=0)
            me = here[(m + 2) % 3]
            for d in (1, 3, 2):
                copy = line_copy(m, d, g2.at[m], u3.at[m, me])
                copy.start()
                pending.append(copy)
            u3[m, me] = g2[m]
        for m in range(3):
            me = here[(m + 2) % 3]
            for d in (1, 3, 2):
                slot = u3.at[m, wrap(me - d)]
                line_copy(m, d, slot, slot).wait_recv()
            h0[m, here[m], here[(m + 1) % 3]] = (u3[m, 0] + u3[m, 1]) + (u3[m, 2] + u3[m, 3])
            each(m, lambda k, i, j: spread_send(m, k, i, j).start())
        owner_in = permute(qp, q, to_owner, 1)

        def join(m, half):
            return remote(gf.at[half, m], gf.at[half, m], ar_send.at[107 + m], ar_recv.at[107 + m], other_core)

        def land(m):
            def landed(k, i, j):
                slot = h0.at[m, wrap(i - k // 4), wrap(j - k % 4)]
                plane_copy(48, m, k, slot, slot).wait_recv()

            each(m, landed)
            gf[core, m] = h0[m].reshape(HALF, SIDE)
            join(m, core).start()

        def joined(m):
            join(m, 1 - core).wait_recv()
            full[m, :HALF] = gf[0, m]
            full[m, HALF:] = gf[1, m]

        first = it == 0
        later = it > 0
        land(0)
        pl.when(first)(lambda: land(1))
        joined(0)

        @pl.when(first)
        def _():
            joined(1)
            norm[...] = full[1]

        raw = full[0]
        mat[...] = jnp.where(core == 0, 0.5 * (raw + raw.T), norm[...])
        head = eliminate(mat[:HALF, :HALF], HALF)
        t = mm(mat[HALF:, :HALF], head)
        corner = mat[HALF:, HALF:] - mm(t, mat[:HALF, HALF:])
        tri[...] = t
        work[...] = corner
        mat[:HALF, :HALF] = head
        pl.when(later)(lambda: land(1))
        land(2)
        tail = eliminate(work[...], HALF)
        t = tri[...]
        low = mm(tail, t)
        inv[core, :HALF, :HALF] = mat[:HALF, :HALF] + mm_t(t, low)
        inv[core, HALF:, :HALF] = -low
        inv[core, :HALF, HALF:] = -low.T
        inv[core, HALF:, HALF:] = tail
        share = remote(inv.at[core], inv.at[core], ar_send.at[106], ar_recv.at[106], other_core)
        share.start()
        pl.when(later)(lambda: joined(1))
        joined(2)
        cross = jnp.where(first, full[0], full[1])
        for copy in pending:
            copy.wait_send()
        for m in range(3):
            join(m, core).wait_send()
            each(m, lambda k, i, j: reduce_send(m, k, i, j).wait_send())
            each(m, lambda k, i, j: spread_send(m, k, i, j).wait_send())
        remote(inv.at[1 - core], inv.at[1 - core], ar_send.at[106], ar_recv.at[106], other_core).wait_recv()
        alpha = mm(inv[0], norm[...])
        fall = mm(cross, alpha)
        after = norm[...] - fall - fall.T + mm_t(alpha, mm(full[2], alpha))
        beta = mm(inv[1], after)
        norm[...] = after
        small[0] = alpha
        small[1] = beta

        permute_wait(owner_in)
        r_ref[...] -= mm(q[...], alpha)
        dold[...] = d_ref[...]
        d_ref[...] = r_ref[...] + mm(d_ref[...], beta)
        share.wait_send()
        return carry

    lax.fori_loop(0, ITERS, iteration, 0)
    x_ref[...] += mm(dold[...], small[0])


def body(covariance, right_side):
    rows, cols = covariance.shape
    piece, side = right_side.shape
    vec = jax.ShapeDtypeStruct((piece, side), F32)
    vmem = pl.BlockSpec(memory_space=pltpu.VMEM)

    def f32(*shape):
        return pltpu.VMEM(shape, F32)

    def dma(n):
        return pltpu.SemaphoreType.DMA((n,))

    out = pl.pallas_call(
        kernel,
        out_shape=(vec, vec, vec),
        in_specs=[pl.BlockSpec(memory_space=pl.ANY), vmem],
        out_specs=(vmem, vmem, vmem),
        scratch_shapes=[
            pltpu.VMEM((8, piece, cols), BF16),
            pltpu.VMEM((4, 4, 2, piece // 2, side), BF16),
            f32(8, piece, side),
            f32(4, piece, side),
            pltpu.VMEM((3, piece, side), WIRE),
            pltpu.VMEM((3, piece, side), WIRE),
            f32(piece, side), f32(piece, side), f32(piece, side), f32(piece, side), f32(piece, side),
            f32(3, side, side), f32(3, HALF, side), f32(3, 4, 4, 8, side), f32(3, 4, 4, 8, side),
            f32(3, 8, side), f32(3, 4, 8, side), f32(3, 4, 4, 8, side), f32(2, 3, HALF, side),
            f32(side, side), f32(3, side, side), f32(2, side, side),
            f32(side, side), f32(HALF, HALF), f32(HALF, HALF), f32(2, side, side),
            pltpu.SemaphoreType.DMA,
            dma(30), dma(30), dma(7), dma(7), dma(2), dma(2), dma(110), dma(110),
        ],
        compiler_params=pltpu.CompilerParams(
            collective_id=0, has_side_effects=True, vmem_limit_bytes=60 * 1024 * 1024
        ),
    )(covariance.reshape(8, piece, cols), right_side)

    def hand_over(*refs):
        for src, dst in zip(refs[:3], refs[3:]):
            dst[...] = src[...]

    return pl.pallas_call(hand_over, out_shape=(vec, vec, vec))(*out)


def solution(mesh):
    spec = P(("col", "row"), None)
    return jax.shard_map(
        body,
        mesh=mesh,
        in_specs=(P("row", "col"), spec),
        out_specs=(spec, spec, spec),
        check_vma=False,
    )
```

```python
import functools

import jax
import jax.numpy as jnp
from jax import lax
from jax.experimental import pallas as pl
from jax.experimental.pallas import tpu as pltpu
from jax.sharding import PartitionSpec as P

ITERS = 3
MESH = pl.DeviceIdType.MESH
HIGHEST = lax.Precision.HIGHEST
F32 = jnp.float32
BF16 = jnp.bfloat16
WIRE = jnp.bfloat16
SIDE = 256
HALF = SIDE // 2
RING = 4
OFFS = (0, -1, 1, 2)


def mm(left, right):
    return jnp.dot(left, right, precision=HIGHEST, preferred_element_type=F32)


def mm_t(left, right):
    return lax.dot_general(
        left, right, (((0,), (0,)), ((), ())), precision=HIGHEST, preferred_element_type=F32
    )


def eliminate(mat, size):
    sub = lax.broadcasted_iota(jnp.int32, (8, size), 0)
    lane = lax.broadcasted_iota(jnp.int32, (8, size), 1)
    tiles = [mat[8 * t : 8 * t + 8, :] for t in range(size // 8)]
    lower, scaled = [], []
    for k in range(0, size, 4):
        p, o = k // 8, k % 8
        inside = (lane >= k) & (lane < k + 4)
        live = range(p if o == 0 else p + 1, size // 8)
        col = {
            i: [jnp.broadcast_to(tiles[i][:, k + j : k + j + 1], (8, size)) for j in range(4)]
            for i in sorted({p, *live})
        }
        e = [[col[p][j][o + i : o + i + 1, :] for j in range(4)] for i in range(4)]
        pivot = jnp.where(inside, jnp.where(lane - k == sub - o, 1.0, 0.0), tiles[p])
        r = [pivot[o + j : o + j + 1, :] for j in range(4)]
        a0, a1, a2 = e[0][0], e[0][1], e[1][1]
        da = 1.0 / (a0 * a2 - a1 * a1)
        u = [
            [a2 * e[0][2] - a1 * e[1][2], a2 * e[0][3] - a1 * e[1][3]],
            [a0 * e[1][2] - a1 * e[0][2], a0 * e[1][3] - a1 * e[0][3]],
        ]
        s0 = e[2][2] - (e[0][2] * u[0][0] + e[1][2] * u[1][0]) * da
        s1 = e[2][3] - (e[0][2] * u[0][1] + e[1][2] * u[1][1]) * da
        s2 = e[3][3] - (e[0][3] * u[0][1] + e[1][3] * u[1][1]) * da
        t = [[v * da for v in w] for w in u]
        ds = 1.0 / (s0 * s2 - s1 * s1)
        w0 = r[2] - t[0][0] * r[0] - t[1][0] * r[1]
        w1 = r[3] - t[0][1] * r[0] - t[1][1] * r[1]
        q0 = (a2 * r[0] - a1 * r[1]) * da
        q1 = (a0 * r[1] - a1 * r[0]) * da
        b0 = (s2 * w0 - s1 * w1) * ds
        b1 = (s0 * w1 - s1 * w0) * ds
        rows = [q0 - (t[0][0] * b0 + t[0][1] * b1), q1 - (t[1][0] * b0 + t[1][1] * b1), b0, b1]
        rows = [jnp.broadcast_to(v, (8, size)) for v in rows]
        left = lane < k + 4
        piece = jnp.where(sub == o, rows[0], jnp.where(sub == o + 1, rows[1], jnp.where(sub == o + 2, rows[2], rows[3])))
        pivot, piece = jnp.where(left, pivot, 0.0), jnp.where(left, piece, 0.0)
        if o == 0:
            lower.append(pivot)
            scaled.append(piece)
        else:
            lower[p] = jnp.where(sub < 4, lower[p], pivot)
            scaled[p] = jnp.where(sub < 4, scaled[p], piece)
        for i in live:
            c, v = col[i], jnp.where(inside, 0.0, tiles[i])
            tiles[i] = (v - c[0] * rows[0] - c[1] * rows[1]) - (c[2] * rows[2] + c[3] * rows[3])
    return mm_t(jnp.concatenate(lower, axis=0), jnp.concatenate(scaled, axis=0))


def kernel(
    a_hbm, b_ref, x_ref, r_ref, d_ref,
    a, lb, part, t1, s3, t3, rp, dp, qp, q, dold,
    g, gt, g0, u1, g2, u3, h0, gf, norm, full, inv, mat, work, tri, small,
    a_sem, ag_send, ag_recv, rs_send, rs_recv, pm_send, pm_recv, ar_send, ar_recv,
):
    row, col = lax.axis_index("row"), lax.axis_index("col")
    z, y, x, core = row // RING, row % RING, col // 2, col % 2
    here = (x, y, z)

    def wrap(v):
        return (v + 2 * RING) % RING

    def device(pos, c):
        return (pos[2] * RING + pos[1], pos[0] * 2 + c)

    def along(axis, d):
        pos = list(here)
        pos[axis] = wrap(pos[axis] + d)
        return device(pos, core)

    other_core = device(here, 1 - core)

    def in_plane(m, d, f):
        pos = list(here)
        pos[m] = wrap(pos[m] + d)
        pos[(m + 1) % 3] = wrap(pos[(m + 1) % 3] + f)
        return device(pos, core)

    def remote(src, dst, send, recv, target):
        return pltpu.make_async_remote_copy(
            src_ref=src, dst_ref=dst, send_sem=send, recv_sem=recv, device_id=target, device_id_type=MESH
        )

    load_a = pltpu.make_async_copy(a_hbm, a, a_sem)
    load_a.start()

    piece_out = col * 16 + row
    to_rows = (piece_out // 8, piece_out % 8)
    piece_in = row * 8 + col
    to_owner = (piece_in % 16, piece_in // 16)
    fixed = piece_out == piece_in

    barrier = pltpu.get_barrier_semaphore()

    def greet(target):
        pl.semaphore_signal(barrier, inc=1, device_id=target, device_id_type=MESH)

    for axis in range(3):
        for d in range(1, RING):
            greet(along(axis, d))
    greet(other_core)
    for m in range(3):
        for d in range(1, RING):
            for f in range(1, RING):
                greet(in_plane(m, d, f))

    @pl.when(jnp.logical_not(fixed))
    def _():
        greet(to_rows)
        greet(to_owner)

    pl.semaphore_wait(barrier, jnp.where(fixed, 37, 39))

    def owner_copy(part_):
        rows = pl.ds(112 * part_, 112)
        return remote(qp.at[rows], q.at[rows], pm_send.at[1 + part_], pm_recv.at[1 + part_], to_owner)

    def owner_start(part_):
        @pl.when(jnp.logical_not(fixed))
        def _():
            owner_copy(part_).start()

        @pl.when(fixed)
        def _():
            rows = pl.ds(112 * part_, 112)
            pltpu.make_async_copy(qp.at[rows], q.at[rows], pm_recv.at[1 + part_]).start()

    def settle(copy):
        copy.wait_recv()

        @pl.when(jnp.logical_not(fixed))
        def _():
            copy.wait_send()

    rows_in = remote(b_ref, rp, pm_send.at[0], pm_recv.at[0], to_rows)

    r_ref[...] = b_ref[...]
    d_ref[...] = b_ref[...]
    x_ref[...] = jnp.zeros_like(x_ref)

    def region(h, c1, c2):
        zc, yc = (c2, c1) if h == 0 else (c1, c2)
        return lb.at[zc, yc, h]

    def gather(h, g_, e, incoming):
        axes = (1, 2) if h == 0 else (2, 1)
        mine = (here[axes[0]], here[axes[1]])
        off = (-1, 1, 2)[e] if incoming else 0
        if g_ == 0:
            c1, c2, axis = wrap(mine[0] + off), mine[1], axes[0]
        else:
            c1, c2, axis = wrap(mine[0] + OFFS[g_ - 1]), wrap(mine[1] + off), axes[1]
        ref = region(h, c1, c2)
        n = h * 15 + g_ * 3 + e
        return remote(ref, ref, ag_send.at[n], ag_recv.at[n], along(axis, (1, -1, 2)[e]))

    def send(h, g_):
        for e in range(3):
            gather(h, g_, e, False).start()

    def take(h, g_, es=(0, 1, 2)):
        for e in es:
            gather(h, g_, e, True).wait_recv()

    def product(zc, j, first):
        cols = pl.ds(pl.multiple_of(zc * 896, 128), 896)
        block = lb[zc].reshape(896, SIDE)
        out = jnp.dot(a[j, :, cols], block, preferred_element_type=F32)
        if first:
            part[j] = out
        else:
            part[j] += out

    def all_products(zc, first):
        def body(j, carry):
            product(zc, j, first)
            return carry

        lax.fori_loop(0, 8, body, 0)

    def shift(i):
        if isinstance(i, int):
            return (2, 1, -1, 0)[i]
        return jnp.where(i == 0, 2, jnp.where(i == 1, 1, jnp.where(i == 2, -1, 0)))

    def core_copy(i):
        j = 2 * wrap(x + shift(i)) + 1 - core
        return remote(part.at[j], t1.at[i], rs_send.at[i], rs_recv.at[i], other_core)

    def ring_copy(i):
        return remote(s3.at[i], t3.at[i], rs_send.at[4 + i], rs_recv.at[4 + i], along(0, shift(i)))

    def plane_copy(base, m, k, src, dst):
        n = base + 16 * m + k
        return remote(src, dst, ar_send.at[n], ar_recv.at[n], in_plane(m, k // 4, k % 4))

    def line_copy(m, d, src, dst):
        n = 96 + 3 * m + d - 1
        return remote(src, dst, ar_send.at[n], ar_recv.at[n], along((m + 2) % 3, d))

    def iteration(it, carry):
        lb[z, y] = d_ref[...].astype(BF16).reshape(2, 112, SIDE)
        for g_ in (0, 1):
            for h in (0, 1):
                send(h, g_)


        @pl.when(it > 0)
        def _():
            rp[...] = rp[...] - mm(qp[...], small[0])
            dp[...] = rp[...] + mm(dp[...], small[1])

        for k in range(3):
            for h in (0, 1):
                take(h, 0, (k,))
                send(h, k + 2)

        @pl.when(it == 0)
        def _():
            @pl.when(jnp.logical_not(fixed))
            def _():
                rows_in.start()

            @pl.when(fixed)
            def _():
                pltpu.make_async_copy(b_ref, rp, pm_recv.at[0]).start()

            load_a.wait()

        @pl.when(it > 0)
        def _():
            x_ref[...] += mm(dold[...], small[0])

        take(1, 1)
        all_products(z, True)
        for k in (1, 2):
            for g_ in (1, 2, 3, 4):
                take(0, g_, (k - 1,))
            take(1, k + 1)
            all_products(wrap(z + OFFS[k]), False)
        for g_ in (1, 2, 3, 4):
            take(0, g_, (2,))
        take(1, 4)

        last = wrap(z + 2)

        def finish(i, c_):
            j = 2 * wrap(x + shift(i)) + 1 - core
            product(last, j, False)
            core_copy(i).start()
            product(last, 2 * wrap(x + shift(i)) + core, False)
            return c_

        lax.fori_loop(0, 4, finish, 0)

        def chip_sum(i):
            core_copy(i).wait_recv()
            return part[2 * wrap(x + shift(i)) + core] + t1[i]

        for i in range(3):
            s3[i] = chip_sum(i).astype(WIRE)
            ring_copy(i).start()
        own = chip_sum(3)
        for h in (0, 1):
            for g_ in range(5):
                for e in range(3):
                    gather(h, g_, e, False).wait_send()
        for i in range(3):
            ring_copy(i).wait_recv()
        qp[...] = own + (t3[0].astype(F32) + t3[1].astype(F32) + t3[2].astype(F32))

        @pl.when(it == 0)
        def _():
            settle(rows_in)
            dp[...] = rp[...]

        image, res = qp[...], rp[...]
        g[0] = mm_t(dp[...], image)
        g[1] = mm_t(res, jnp.where(it == 0, res, image))
        g[2] = mm_t(image, image)
        theirs = pl.ds(pl.multiple_of((1 - core) * HALF, HALF), HALF)
        ours = pl.ds(pl.multiple_of(core * HALF, HALF), HALF)
        swap = remote(g.at[:, theirs], gt, ar_send.at[105], ar_recv.at[105], other_core)
        swap.start()
        for i in range(4):
            core_copy(i).wait_send()
        for i in range(3):
            ring_copy(i).wait_send()
        swap.wait_recv()
        g0[...] = (g[:, ours] + gt[...]).reshape(3, RING, RING, 8, SIDE)
        pending = [swap]

        def each(m, fn):
            i, j = here[m], here[(m + 1) % 3]

            def step(k, c_):
                fn(k, i, j)
                return c_

            lax.fori_loop(1, 16, step, 0)

        def reduce_send(m, k, i, j):
            src = g0.at[m, wrap(i + k // 4), wrap(j + k % 4)]
            return plane_copy(0, m, k, src, u1.at[m, i, j])

        def spread_send(m, k, i, j):
            return plane_copy(48, m, k, h0.at[m, i, j], h0.at[m, i, j])

        for m in range(3):
            each(m, lambda k, i, j: reduce_send(m, k, i, j).start())
            i, j = here[m], here[(m + 1) % 3]
            u1[m, i, j] = g0[m, i, j]
        for m in range(3):
            def arrived(k, i, j):
                slot = u1.at[m, wrap(i - k // 4), wrap(j - k % 4)]
                plane_copy(0, m, k, slot, slot).wait_recv()

            each(m, arrived)
            g2[m] = jnp.sum(u1[m].reshape(16, 8, SIDE), axis=0)
            me = here[(m + 2) % 3]
            for d in (1, 3, 2):
                copy = line_copy(m, d, g2.at[m], u3.at[m, me])
                copy.start()
                pending.append(copy)
            u3[m, me] = g2[m]
        for m in range(3):
            me = here[(m + 2) % 3]
            for d in (1, 3, 2):
                slot = u3.at[m, wrap(me - d)]
                line_copy(m, d, slot, slot).wait_recv()
            h0[m, here[m], here[(m + 1) % 3]] = (u3[m, 0] + u3[m, 1]) + (u3[m, 2] + u3[m, 3])
            each(m, lambda k, i, j: spread_send(m, k, i, j).start())

        def join(m, half):
            return remote(gf.at[half, m], gf.at[half, m], ar_send.at[107 + m], ar_recv.at[107 + m], other_core)

        def land(m):
            def landed(k, i, j):
                slot = h0.at[m, wrap(i - k // 4), wrap(j - k % 4)]
                plane_copy(48, m, k, slot, slot).wait_recv()

            each(m, landed)
            gf[core, m] = h0[m].reshape(HALF, SIDE)
            join(m, core).start()

        def joined(m):
            join(m, 1 - core).wait_recv()
            full[m, :HALF] = gf[0, m]
            full[m, HALF:] = gf[1, m]

        first = it == 0
        later = it > 0
        land(0)
        pl.when(first)(lambda: land(1))
        joined(0)

        @pl.when(first)
        def _():
            joined(1)
            norm[...] = full[1]

        owner_start(0)
        owner_start(1)
        raw = full[0]
        mat[...] = jnp.where(core == 0, 0.5 * (raw + raw.T), norm[...])
        head = eliminate(mat[:HALF, :HALF], HALF)
        t = mm(mat[HALF:, :HALF], head)
        corner = mat[HALF:, HALF:] - mm(t, mat[:HALF, HALF:])
        tri[...] = t
        work[...] = corner
        mat[:HALF, :HALF] = head
        pl.when(later)(lambda: land(1))
        land(2)
        tail = eliminate(work[...], HALF)
        t = tri[...]
        low = mm(tail, t)
        inv[core, :HALF, :HALF] = mat[:HALF, :HALF] + mm_t(t, low)
        inv[core, HALF:, :HALF] = -low
        inv[core, :HALF, HALF:] = -low.T
        inv[core, HALF:, HALF:] = tail
        share = remote(inv.at[core], inv.at[core], ar_send.at[106], ar_recv.at[106], other_core)
        share.start()
        pl.when(later)(lambda: joined(1))
        joined(2)
        cross = jnp.where(first, full[0], full[1])
        for copy in pending:
            copy.wait_send()
        for m in range(3):
            join(m, core).wait_send()
            each(m, lambda k, i, j: reduce_send(m, k, i, j).wait_send())
            each(m, lambda k, i, j: spread_send(m, k, i, j).wait_send())
        remote(inv.at[1 - core], inv.at[1 - core], ar_send.at[106], ar_recv.at[106], other_core).wait_recv()
        alpha = mm(inv[0], norm[...])
        fall = mm(cross, alpha)
        after = norm[...] - fall - fall.T + mm_t(alpha, mm(full[2], alpha))
        beta = mm(inv[1], after)
        norm[...] = after
        small[0] = alpha
        small[1] = beta

        settle(owner_copy(0))
        settle(owner_copy(1))
        r_ref[...] -= mm(q[...], alpha)
        dold[...] = d_ref[...]
        d_ref[...] = r_ref[...] + mm(d_ref[...], beta)
        share.wait_send()
        return carry

    lax.fori_loop(0, ITERS, iteration, 0)
    x_ref[...] += mm(dold[...], small[0])


def body(covariance, right_side):
    rows, cols = covariance.shape
    piece, side = right_side.shape
    vec = jax.ShapeDtypeStruct((piece, side), F32)
    vmem = pl.BlockSpec(memory_space=pltpu.VMEM)

    def f32(*shape):
        return pltpu.VMEM(shape, F32)

    def dma(n):
        return pltpu.SemaphoreType.DMA((n,))

    out = pl.pallas_call(
        kernel,
        out_shape=(vec, vec, vec),
        in_specs=[pl.BlockSpec(memory_space=pl.ANY), vmem],
        out_specs=(vmem, vmem, vmem),
        scratch_shapes=[
            pltpu.VMEM((8, piece, cols), BF16),
            pltpu.VMEM((4, 4, 2, piece // 2, side), BF16),
            f32(8, piece, side),
            f32(4, piece, side),
            pltpu.VMEM((3, piece, side), WIRE),
            pltpu.VMEM((3, piece, side), WIRE),
            f32(piece, side), f32(piece, side), f32(piece, side), f32(piece, side), f32(piece, side),
            f32(3, side, side), f32(3, HALF, side), f32(3, 4, 4, 8, side), f32(3, 4, 4, 8, side),
            f32(3, 8, side), f32(3, 4, 8, side), f32(3, 4, 4, 8, side), f32(2, 3, HALF, side),
            f32(side, side), f32(3, side, side), f32(2, side, side),
            f32(side, side), f32(HALF, HALF), f32(HALF, HALF), f32(2, side, side),
            pltpu.SemaphoreType.DMA,
            dma(30), dma(30), dma(7), dma(7), dma(3), dma(3), dma(110), dma(110),
        ],
        compiler_params=pltpu.CompilerParams(
            collective_id=0, has_side_effects=True, vmem_limit_bytes=60 * 1024 * 1024
        ),
    )(covariance.reshape(8, piece, cols), right_side)

    def hand_over(*refs):
        for src, dst in zip(refs[:3], refs[3:]):
            dst[...] = src[...]

    return pl.pallas_call(hand_over, out_shape=(vec, vec, vec))(*out)


def solution(mesh):
    spec = P(("col", "row"), None)
    return jax.shard_map(
        body,
        mesh=mesh,
        in_specs=(P("row", "col"), spec),
        out_specs=(spec, spec, spec),
        check_vma=False,
    )
```

```python
import functools

import jax
import jax.numpy as jnp
from jax import lax
from jax.experimental import pallas as pl
from jax.experimental.pallas import tpu as pltpu
from jax.sharding import PartitionSpec as P

ITERS = 3
MESH = pl.DeviceIdType.MESH
HIGHEST = lax.Precision.HIGHEST
F32 = jnp.float32
BF16 = jnp.bfloat16
WIRE = jnp.bfloat16
SIDE = 256
HALF = SIDE // 2
RING = 4
OFFS = (0, -1, 1, 2)


def mm(left, right):
    return jnp.dot(left, right, precision=HIGHEST, preferred_element_type=F32)


def mm_t(left, right):
    return lax.dot_general(
        left, right, (((0,), (0,)), ((), ())), precision=HIGHEST, preferred_element_type=F32
    )


def eliminate(mat, size):
    sub = lax.broadcasted_iota(jnp.int32, (8, size), 0)
    lane = lax.broadcasted_iota(jnp.int32, (8, size), 1)
    tiles = [mat[8 * t : 8 * t + 8, :] for t in range(size // 8)]
    lower, scaled = [], []
    for k in range(0, size, 4):
        p, o = k // 8, k % 8
        inside = (lane >= k) & (lane < k + 4)
        live = range(p if o == 0 else p + 1, size // 8)
        col = {
            i: [jnp.broadcast_to(tiles[i][:, k + j : k + j + 1], (8, size)) for j in range(4)]
            for i in sorted({p, *live})
        }
        e = [[col[p][j][o + i : o + i + 1, :] for j in range(4)] for i in range(4)]
        pivot = jnp.where(inside, jnp.where(lane - k == sub - o, 1.0, 0.0), tiles[p])
        r = [pivot[o + j : o + j + 1, :] for j in range(4)]
        a0, a1, a2 = e[0][0], e[0][1], e[1][1]
        da = 1.0 / (a0 * a2 - a1 * a1)
        u = [
            [a2 * e[0][2] - a1 * e[1][2], a2 * e[0][3] - a1 * e[1][3]],
            [a0 * e[1][2] - a1 * e[0][2], a0 * e[1][3] - a1 * e[0][3]],
        ]
        s0 = e[2][2] - (e[0][2] * u[0][0] + e[1][2] * u[1][0]) * da
        s1 = e[2][3] - (e[0][2] * u[0][1] + e[1][2] * u[1][1]) * da
        s2 = e[3][3] - (e[0][3] * u[0][1] + e[1][3] * u[1][1]) * da
        t = [[v * da for v in w] for w in u]
        ds = 1.0 / (s0 * s2 - s1 * s1)
        w0 = r[2] - t[0][0] * r[0] - t[1][0] * r[1]
        w1 = r[3] - t[0][1] * r[0] - t[1][1] * r[1]
        q0 = (a2 * r[0] - a1 * r[1]) * da
        q1 = (a0 * r[1] - a1 * r[0]) * da
        b0 = (s2 * w0 - s1 * w1) * ds
        b1 = (s0 * w1 - s1 * w0) * ds
        rows = [q0 - (t[0][0] * b0 + t[0][1] * b1), q1 - (t[1][0] * b0 + t[1][1] * b1), b0, b1]
        rows = [jnp.broadcast_to(v, (8, size)) for v in rows]
        left = lane < k + 4
        piece = jnp.where(sub == o, rows[0], jnp.where(sub == o + 1, rows[1], jnp.where(sub == o + 2, rows[2], rows[3])))
        pivot, piece = jnp.where(left, pivot, 0.0), jnp.where(left, piece, 0.0)
        if o == 0:
            lower.append(pivot)
            scaled.append(piece)
        else:
            lower[p] = jnp.where(sub < 4, lower[p], pivot)
            scaled[p] = jnp.where(sub < 4, scaled[p], piece)
        for i in live:
            c, v = col[i], jnp.where(inside, 0.0, tiles[i])
            tiles[i] = (v - c[0] * rows[0] - c[1] * rows[1]) - (c[2] * rows[2] + c[3] * rows[3])
    return mm_t(jnp.concatenate(lower, axis=0), jnp.concatenate(scaled, axis=0))


def kernel(
    a_hbm, b_ref, x_ref, r_ref, d_ref,
    a, lb, part, t1, s3, t3, rp, dp, qp, q, dold,
    g, gt, g0, u1, g2, u3, h0, gf, norm, full, inv, mat, work, tri, small,
    a_sem, ag_send, ag_recv, rs_send, rs_recv, pm_send, pm_recv, ar_send, ar_recv,
):
    row, col = lax.axis_index("row"), lax.axis_index("col")
    z, y, x, core = row // RING, row % RING, col // 2, col % 2
    here = (x, y, z)

    def wrap(v):
        return (v + 2 * RING) % RING

    def device(pos, c):
        return (pos[2] * RING + pos[1], pos[0] * 2 + c)

    def along(axis, d):
        pos = list(here)
        pos[axis] = wrap(pos[axis] + d)
        return device(pos, core)

    other_core = device(here, 1 - core)

    def in_plane(m, d, f):
        pos = list(here)
        pos[m] = wrap(pos[m] + d)
        pos[(m + 1) % 3] = wrap(pos[(m + 1) % 3] + f)
        return device(pos, core)

    def remote(src, dst, send, recv, target):
        return pltpu.make_async_remote_copy(
            src_ref=src, dst_ref=dst, send_sem=send, recv_sem=recv, device_id=target, device_id_type=MESH
        )

    load_a = pltpu.make_async_copy(a_hbm, a, a_sem)
    load_a.start()

    piece_out = col * 16 + row
    row_out, slot_out = piece_out // 8, piece_out % 8
    to_rows = (row_out, 2 * wrap(slot_out // 2 + row_out // RING) + slot_out % 2)
    piece_in = row * 8 + 2 * wrap(x - z) + core
    to_owner = (piece_in % 16, piece_in // 16)
    fixed = piece_out == piece_in

    barrier = pltpu.get_barrier_semaphore()

    def greet(target):
        pl.semaphore_signal(barrier, inc=1, device_id=target, device_id_type=MESH)

    for axis in range(3):
        for d in range(1, RING):
            greet(along(axis, d))
    greet(other_core)
    for m in range(3):
        for d in range(1, RING):
            for f in range(1, RING):
                greet(in_plane(m, d, f))

    @pl.when(jnp.logical_not(fixed))
    def _():
        greet(to_rows)
        greet(to_owner)

    pl.semaphore_wait(barrier, jnp.where(fixed, 37, 39))

    def owner_copy(part_):
        rows = pl.ds(112 * part_, 112)
        return remote(qp.at[rows], q.at[rows], pm_send.at[1 + part_], pm_recv.at[1 + part_], to_owner)

    def owner_start(part_):
        @pl.when(jnp.logical_not(fixed))
        def _():
            owner_copy(part_).start()

        @pl.when(fixed)
        def _():
            rows = pl.ds(112 * part_, 112)
            pltpu.make_async_copy(qp.at[rows], q.at[rows], pm_recv.at[1 + part_]).start()

    def settle(copy):
        copy.wait_recv()

        @pl.when(jnp.logical_not(fixed))
        def _():
            copy.wait_send()

    rows_in = remote(b_ref, rp, pm_send.at[0], pm_recv.at[0], to_rows)

    r_ref[...] = b_ref[...]
    d_ref[...] = b_ref[...]
    x_ref[...] = jnp.zeros_like(x_ref)

    def region(h, c1, c2):
        zc, yc = (c2, c1) if h == 0 else (c1, c2)
        return lb.at[zc, yc, h]

    def gather(h, g_, e, incoming):
        axes = (1, 2) if h == 0 else (2, 1)
        mine = (here[axes[0]], here[axes[1]])
        off = (-1, 1, 2)[e] if incoming else 0
        if g_ == 0:
            c1, c2, axis = wrap(mine[0] + off), mine[1], axes[0]
        else:
            c1, c2, axis = wrap(mine[0] + OFFS[g_ - 1]), wrap(mine[1] + off), axes[1]
        ref = region(h, c1, c2)
        n = h * 15 + g_ * 3 + e
        return remote(ref, ref, ag_send.at[n], ag_recv.at[n], along(axis, (1, -1, 2)[e]))

    def send(h, g_):
        for e in range(3):
            gather(h, g_, e, False).start()

    def take(h, g_, es=(0, 1, 2)):
        for e in es:
            gather(h, g_, e, True).wait_recv()

    def product(zc, j, first):
        cols = pl.ds(pl.multiple_of(zc * 896, 128), 896)
        block = lb[zc].reshape(896, SIDE)
        out = jnp.dot(a[j, :, cols], block, preferred_element_type=F32)
        if first:
            part[j] = out
        else:
            part[j] += out

    def all_products(zc, first):
        def body(j, carry):
            product(zc, j, first)
            return carry

        lax.fori_loop(0, 8, body, 0)

    def shift(i):
        if isinstance(i, int):
            return (2, 1, -1, 0)[i]
        return jnp.where(i == 0, 2, jnp.where(i == 1, 1, jnp.where(i == 2, -1, 0)))

    def part_of(i):
        return wrap(x + shift(i) - z)

    def core_copy(i):
        j = 2 * part_of(i) + 1 - core
        return remote(part.at[j], t1.at[i], rs_send.at[i], rs_recv.at[i], other_core)

    def ring_copy(i):
        return remote(s3.at[i], t3.at[i], rs_send.at[4 + i], rs_recv.at[4 + i], along(0, shift(i)))

    def plane_copy(base, m, k, src, dst):
        n = base + 16 * m + k
        return remote(src, dst, ar_send.at[n], ar_recv.at[n], in_plane(m, k // 4, k % 4))

    def line_copy(m, d, src, dst):
        n = 96 + 3 * m + d - 1
        return remote(src, dst, ar_send.at[n], ar_recv.at[n], along((m + 2) % 3, d))

    def iteration(it, carry):
        lb[z, y] = d_ref[...].astype(BF16).reshape(2, 112, SIDE)
        for g_ in (0, 1):
            for h in (0, 1):
                send(h, g_)


        @pl.when(it > 0)
        def _():
            rp[...] = rp[...] - mm(qp[...], small[0])
            dp[...] = rp[...] + mm(dp[...], small[1])

        for k in range(3):
            for h in (0, 1):
                take(h, 0, (k,))
                send(h, k + 2)

        @pl.when(it == 0)
        def _():
            @pl.when(jnp.logical_not(fixed))
            def _():
                rows_in.start()

            @pl.when(fixed)
            def _():
                pltpu.make_async_copy(b_ref, rp, pm_recv.at[0]).start()

            load_a.wait()

        @pl.when(it > 0)
        def _():
            x_ref[...] += mm(dold[...], small[0])

        take(1, 1)
        all_products(z, True)
        for k in (1, 2):
            for g_ in (1, 2, 3, 4):
                take(0, g_, (k - 1,))
            take(1, k + 1)
            all_products(wrap(z + OFFS[k]), False)
        for g_ in (1, 2, 3, 4):
            take(0, g_, (2,))
        take(1, 4)

        last = wrap(z + 2)

        def finish(i, c_):
            j = 2 * part_of(i) + 1 - core
            product(last, j, False)
            core_copy(i).start()
            product(last, 2 * part_of(i) + core, False)
            return c_

        lax.fori_loop(0, 4, finish, 0)

        def chip_sum(i):
            core_copy(i).wait_recv()
            return part[2 * part_of(i) + core] + t1[i]

        for i in range(3):
            s3[i] = chip_sum(i).astype(WIRE)
            ring_copy(i).start()
        own = chip_sum(3)
        for h in (0, 1):
            for g_ in range(5):
                for e in range(3):
                    gather(h, g_, e, False).wait_send()
        for i in range(3):
            ring_copy(i).wait_recv()
        qp[...] = own + (t3[0].astype(F32) + t3[1].astype(F32) + t3[2].astype(F32))

        @pl.when(it == 0)
        def _():
            settle(rows_in)
            dp[...] = rp[...]

        image, res = qp[...], rp[...]
        theirs = pl.ds(pl.multiple_of((1 - core) * HALF, HALF), HALF)
        ours = pl.ds(pl.multiple_of(core * HALF, HALF), HALF)

        def swap(m):
            return remote(g.at[m, theirs], gt.at[m], ar_send.at[110 + m], ar_recv.at[110 + m], other_core)

        g[0] = mm_t(dp[...], image)
        swap(0).start()
        g[1] = mm_t(res, jnp.where(it == 0, res, image))
        swap(1).start()
        g[2] = mm_t(image, image)
        swap(2).start()
        for i in range(4):
            core_copy(i).wait_send()
        for i in range(3):
            ring_copy(i).wait_send()
        pending = []

        def each(m, fn):
            i, j = here[m], here[(m + 1) % 3]

            def step(k, c_):
                fn(k, i, j)
                return c_

            lax.fori_loop(1, 16, step, 0)

        def reduce_send(m, k, i, j):
            src = g0.at[m, wrap(i + k // 4), wrap(j + k % 4)]
            return plane_copy(0, m, k, src, u1.at[m, i, j])

        def spread_send(m, k, i, j):
            return plane_copy(48, m, k, h0.at[m, i, j], h0.at[m, i, j])

        for m in range(3):
            swap(m).wait_recv()
            g0[m] = (g[m, ours] + gt[m]).reshape(RING, RING, 8, SIDE)
            each(m, lambda k, i, j: reduce_send(m, k, i, j).start())
            i, j = here[m], here[(m + 1) % 3]
            u1[m, i, j] = g0[m, i, j]
        for m in range(3):
            def arrived(k, i, j):
                slot = u1.at[m, wrap(i - k // 4), wrap(j - k % 4)]
                plane_copy(0, m, k, slot, slot).wait_recv()

            each(m, arrived)
            g2[m] = jnp.sum(u1[m].reshape(16, 8, SIDE), axis=0)
            me = here[(m + 2) % 3]
            for d in (1, 3, 2):
                copy = line_copy(m, d, g2.at[m], u3.at[m, me])
                copy.start()
                pending.append(copy)
            u3[m, me] = g2[m]
        for m in range(3):
            me = here[(m + 2) % 3]
            for d in (1, 3, 2):
                slot = u3.at[m, wrap(me - d)]
                line_copy(m, d, slot, slot).wait_recv()
            h0[m, here[m], here[(m + 1) % 3]] = (u3[m, 0] + u3[m, 1]) + (u3[m, 2] + u3[m, 3])
            each(m, lambda k, i, j: spread_send(m, k, i, j).start())

        def join(m, half):
            return remote(gf.at[half, m], gf.at[half, m], ar_send.at[107 + m], ar_recv.at[107 + m], other_core)

        def land(m):
            def landed(k, i, j):
                slot = h0.at[m, wrap(i - k // 4), wrap(j - k % 4)]
                plane_copy(48, m, k, slot, slot).wait_recv()

            each(m, landed)
            gf[core, m] = h0[m].reshape(HALF, SIDE)
            join(m, core).start()

        def joined(m):
            join(m, 1 - core).wait_recv()
            full[m, :HALF] = gf[0, m]
            full[m, HALF:] = gf[1, m]

        first = it == 0
        later = it > 0
        land(0)

        @pl.when(first)
        def _():
            land(1)
            joined(1)
            norm[...] = full[1]

        owner_start(0)
        owner_start(1)
        raw = gf[core, 0, :, :HALF]
        head = eliminate(jnp.where(core == 0, 0.5 * (raw + raw.T), norm[:HALF, :HALF]), HALF)
        joined(0)
        raw = full[0]
        mat[...] = jnp.where(core == 0, 0.5 * (raw + raw.T), norm[...])
        t = mm(mat[HALF:, :HALF], head)
        corner = mat[HALF:, HALF:] - mm(t, mat[:HALF, HALF:])
        tri[...] = t
        work[...] = corner
        mat[:HALF, :HALF] = head
        tail = eliminate(work[...], HALF)
        t = tri[...]
        low = mm(tail, t)
        inv[core, :HALF, :HALF] = mat[:HALF, :HALF] + mm_t(t, low)
        inv[core, HALF:, :HALF] = -low
        inv[core, :HALF, HALF:] = -low.T
        inv[core, HALF:, HALF:] = tail
        share = remote(inv.at[core], inv.at[core], ar_send.at[106], ar_recv.at[106], other_core)
        share.start()
        pl.when(later)(lambda: land(1))
        land(2)
        remote(inv.at[1 - core], inv.at[1 - core], ar_send.at[106], ar_recv.at[106], other_core).wait_recv()
        alpha = mm(inv[0], norm[...])
        pl.when(later)(lambda: joined(1))
        joined(2)
        cross = jnp.where(first, full[0], full[1])
        for copy in pending:
            copy.wait_send()
        for m in range(3):
            swap(m).wait_send()
            join(m, core).wait_send()
            each(m, lambda k, i, j: reduce_send(m, k, i, j).wait_send())
            each(m, lambda k, i, j: spread_send(m, k, i, j).wait_send())
        fall = mm(cross, alpha)
        after = norm[...] - fall - fall.T + mm_t(alpha, mm(full[2], alpha))
        beta = mm(inv[1], after)
        norm[...] = after
        small[0] = alpha
        small[1] = beta

        settle(owner_copy(0))
        settle(owner_copy(1))
        r_ref[...] -= mm(q[...], alpha)
        dold[...] = d_ref[...]
        d_ref[...] = r_ref[...] + mm(d_ref[...], beta)
        share.wait_send()
        return carry

    lax.fori_loop(0, ITERS, iteration, 0)
    x_ref[...] += mm(dold[...], small[0])


def body(covariance, right_side):
    rows, cols = covariance.shape
    piece, side = right_side.shape
    vec = jax.ShapeDtypeStruct((piece, side), F32)
    vmem = pl.BlockSpec(memory_space=pltpu.VMEM)

    def f32(*shape):
        return pltpu.VMEM(shape, F32)

    def dma(n):
        return pltpu.SemaphoreType.DMA((n,))

    out = pl.pallas_call(
        kernel,
        out_shape=(vec, vec, vec),
        in_specs=[pl.BlockSpec(memory_space=pl.ANY), vmem],
        out_specs=(vmem, vmem, vmem),
        scratch_shapes=[
            pltpu.VMEM((8, piece, cols), BF16),
            pltpu.VMEM((4, 4, 2, piece // 2, side), BF16),
            f32(8, piece, side),
            f32(4, piece, side),
            pltpu.VMEM((3, piece, side), WIRE),
            pltpu.VMEM((3, piece, side), WIRE),
            f32(piece, side), f32(piece, side), f32(piece, side), f32(piece, side), f32(piece, side),
            f32(3, side, side), f32(3, HALF, side), f32(3, 4, 4, 8, side), f32(3, 4, 4, 8, side),
            f32(3, 8, side), f32(3, 4, 8, side), f32(3, 4, 4, 8, side), f32(2, 3, HALF, side),
            f32(side, side), f32(3, side, side), f32(2, side, side),
            f32(side, side), f32(HALF, HALF), f32(HALF, HALF), f32(2, side, side),
            pltpu.SemaphoreType.DMA,
            dma(30), dma(30), dma(7), dma(7), dma(3), dma(3), dma(113), dma(113),
        ],
        compiler_params=pltpu.CompilerParams(
            collective_id=0, has_side_effects=True, vmem_limit_bytes=60 * 1024 * 1024
        ),
    )(covariance.reshape(8, piece, cols), right_side)

    def hand_over(*refs):
        for src, dst in zip(refs[:3], refs[3:]):
            dst[...] = src[...]

    return pl.pallas_call(hand_over, out_shape=(vec, vec, vec))(*out)


def solution(mesh):
    spec = P(("col", "row"), None)
    return jax.shard_map(
        body,
        mesh=mesh,
        in_specs=(P("row", "col"), spec),
        out_specs=(spec, spec, spec),
        check_vma=False,
    )
```

```python
import functools

import jax
import jax.numpy as jnp
from jax import lax
from jax.experimental import pallas as pl
from jax.experimental.pallas import tpu as pltpu
from jax.sharding import PartitionSpec as P

ITERS = 3
MESH = pl.DeviceIdType.MESH
HIGHEST = lax.Precision.HIGHEST
F32 = jnp.float32
BF16 = jnp.bfloat16
WIRE = jnp.bfloat16
SIDE = 256
HALF = SIDE // 2
RING = 4
OFFS = (0, -1, 1, 2)


def mm(left, right):
    return jnp.dot(left, right, precision=HIGHEST, preferred_element_type=F32)


def mm_t(left, right):
    return lax.dot_general(
        left, right, (((0,), (0,)), ((), ())), precision=HIGHEST, preferred_element_type=F32
    )


def eliminate(mat, size):
    sub = lax.broadcasted_iota(jnp.int32, (8, size), 0)
    lane = lax.broadcasted_iota(jnp.int32, (8, size), 1)
    tiles = [mat[8 * t : 8 * t + 8, :] for t in range(size // 8)]
    lower, scaled = [], []
    for k in range(0, size, 4):
        p, o = k // 8, k % 8
        inside = (lane >= k) & (lane < k + 4)
        live = range(p if o == 0 else p + 1, size // 8)
        col = {
            i: [jnp.broadcast_to(tiles[i][:, k + j : k + j + 1], (8, size)) for j in range(4)]
            for i in sorted({p, *live})
        }
        e = [[col[p][j][o + i : o + i + 1, :] for j in range(4)] for i in range(4)]
        pivot = jnp.where(inside, jnp.where(lane - k == sub - o, 1.0, 0.0), tiles[p])
        r = [pivot[o + j : o + j + 1, :] for j in range(4)]
        a0, a1, a2 = e[0][0], e[0][1], e[1][1]
        da = 1.0 / (a0 * a2 - a1 * a1)
        u = [
            [a2 * e[0][2] - a1 * e[1][2], a2 * e[0][3] - a1 * e[1][3]],
            [a0 * e[1][2] - a1 * e[0][2], a0 * e[1][3] - a1 * e[0][3]],
        ]
        s0 = e[2][2] - (e[0][2] * u[0][0] + e[1][2] * u[1][0]) * da
        s1 = e[2][3] - (e[0][2] * u[0][1] + e[1][2] * u[1][1]) * da
        s2 = e[3][3] - (e[0][3] * u[0][1] + e[1][3] * u[1][1]) * da
        t = [[v * da for v in w] for w in u]
        ds = 1.0 / (s0 * s2 - s1 * s1)
        w0 = r[2] - t[0][0] * r[0] - t[1][0] * r[1]
        w1 = r[3] - t[0][1] * r[0] - t[1][1] * r[1]
        q0 = (a2 * r[0] - a1 * r[1]) * da
        q1 = (a0 * r[1] - a1 * r[0]) * da
        b0 = (s2 * w0 - s1 * w1) * ds
        b1 = (s0 * w1 - s1 * w0) * ds
        rows = [q0 - (t[0][0] * b0 + t[0][1] * b1), q1 - (t[1][0] * b0 + t[1][1] * b1), b0, b1]
        rows = [jnp.broadcast_to(v, (8, size)) for v in rows]
        left = lane < k + 4
        piece = jnp.where(sub == o, rows[0], jnp.where(sub == o + 1, rows[1], jnp.where(sub == o + 2, rows[2], rows[3])))
        pivot, piece = jnp.where(left, pivot, 0.0), jnp.where(left, piece, 0.0)
        if o == 0:
            lower.append(pivot)
            scaled.append(piece)
        else:
            lower[p] = jnp.where(sub < 4, lower[p], pivot)
            scaled[p] = jnp.where(sub < 4, scaled[p], piece)
        for i in live:
            c, v = col[i], jnp.where(inside, 0.0, tiles[i])
            tiles[i] = (v - c[0] * rows[0] - c[1] * rows[1]) - (c[2] * rows[2] + c[3] * rows[3])
    return mm_t(jnp.concatenate(lower, axis=0), jnp.concatenate(scaled, axis=0))


def kernel(
    a_hbm, b_ref, x_ref, r_ref, d_ref,
    a, lb, part, t1, s3, t3, rp, dp, qp, q, dold,
    g, gt, g0, u1, g2, u3, h0, gf, norm, full, inv, mat, work, tri, small,
    a_sem, ag_send, ag_recv, rs_send, rs_recv, pm_send, pm_recv, ar_send, ar_recv,
):
    row, col = lax.axis_index("row"), lax.axis_index("col")
    z, y, x, core = row // RING, row % RING, col // 2, col % 2
    here = (x, y, z)

    def wrap(v):
        return (v + 2 * RING) % RING

    def device(pos, c):
        return (pos[2] * RING + pos[1], pos[0] * 2 + c)

    def along(axis, d):
        pos = list(here)
        pos[axis] = wrap(pos[axis] + d)
        return device(pos, core)

    other_core = device(here, 1 - core)

    def in_plane(m, d, f):
        pos = list(here)
        pos[m] = wrap(pos[m] + d)
        pos[(m + 1) % 3] = wrap(pos[(m + 1) % 3] + f)
        return device(pos, core)

    def remote(src, dst, send, recv, target):
        return pltpu.make_async_remote_copy(
            src_ref=src, dst_ref=dst, send_sem=send, recv_sem=recv, device_id=target, device_id_type=MESH
        )

    load_a = pltpu.make_async_copy(a_hbm, a, a_sem)
    load_a.start()

    piece_out = col * 16 + row
    row_out, slot_out = piece_out // 8, piece_out % 8
    to_rows = (row_out, 2 * wrap(slot_out // 2 + row_out // RING) + slot_out % 2)
    piece_in = row * 8 + 2 * wrap(x - z) + core
    to_owner = (piece_in % 16, piece_in // 16)
    fixed = piece_out == piece_in

    barrier = pltpu.get_barrier_semaphore()

    def greet(target):
        pl.semaphore_signal(barrier, inc=1, device_id=target, device_id_type=MESH)

    for axis in range(3):
        for d in range(1, RING):
            greet(along(axis, d))
    greet(other_core)
    for m in range(3):
        for d in range(1, RING):
            for f in range(1, RING):
                greet(in_plane(m, d, f))

    @pl.when(jnp.logical_not(fixed))
    def _():
        greet(to_rows)
        greet(to_owner)

    pl.semaphore_wait(barrier, jnp.where(fixed, 37, 39))

    def owner_copy(part_):
        rows = pl.ds(112 * part_, 112)
        return remote(qp.at[rows], q.at[rows], pm_send.at[1 + part_], pm_recv.at[1 + part_], to_owner)

    def owner_start(part_):
        @pl.when(jnp.logical_not(fixed))
        def _():
            owner_copy(part_).start()

        @pl.when(fixed)
        def _():
            rows = pl.ds(112 * part_, 112)
            pltpu.make_async_copy(qp.at[rows], q.at[rows], pm_recv.at[1 + part_]).start()

    def settle(copy):
        copy.wait_recv()

        @pl.when(jnp.logical_not(fixed))
        def _():
            copy.wait_send()

    rows_in = remote(b_ref, rp, pm_send.at[0], pm_recv.at[0], to_rows)

    r_ref[...] = b_ref[...]
    d_ref[...] = b_ref[...]
    x_ref[...] = jnp.zeros_like(x_ref)

    def region(h, c1, c2):
        zc, yc = (c2, c1) if h == 0 else (c1, c2)
        return lb.at[zc, yc, h]

    def gather(h, g_, e, incoming):
        axes = (1, 2) if h == 0 else (2, 1)
        mine = (here[axes[0]], here[axes[1]])
        off = (-1, 1, 2)[e] if incoming else 0
        if g_ == 0:
            c1, c2, axis = wrap(mine[0] + off), mine[1], axes[0]
        else:
            c1, c2, axis = wrap(mine[0] + OFFS[g_ - 1]), wrap(mine[1] + off), axes[1]
        ref = region(h, c1, c2)
        n = h * 15 + g_ * 3 + e
        return remote(ref, ref, ag_send.at[n], ag_recv.at[n], along(axis, (1, -1, 2)[e]))

    def send(h, g_):
        for e in range(3):
            gather(h, g_, e, False).start()

    def take(h, g_, es=(0, 1, 2)):
        for e in es:
            gather(h, g_, e, True).wait_recv()

    def product(zc, j, first):
        cols = pl.ds(pl.multiple_of(zc * 896, 128), 896)
        block = lb[zc].reshape(896, SIDE)
        out = jnp.dot(a[j, :, cols], block, preferred_element_type=F32)
        if first:
            part[j] = out
        else:
            part[j] += out

    def all_products(zc, first):
        def body(j, carry):
            product(zc, j, first)
            return carry

        lax.fori_loop(0, 8, body, 0)

    def shift(i):
        if isinstance(i, int):
            return (2, 1, -1, 0)[i]
        return jnp.where(i == 0, 2, jnp.where(i == 1, 1, jnp.where(i == 2, -1, 0)))

    def part_of(i):
        return wrap(x + shift(i) - z)

    def core_copy(i):
        j = 2 * part_of(i) + 1 - core
        return remote(part.at[j], t1.at[i], rs_send.at[i], rs_recv.at[i], other_core)

    def ring_copy(i):
        return remote(s3.at[i], t3.at[i], rs_send.at[4 + i], rs_recv.at[4 + i], along(0, shift(i)))

    def plane_copy(base, m, k, src, dst):
        n = base + 16 * m + k
        return remote(src, dst, ar_send.at[n], ar_recv.at[n], in_plane(m, k // 4, k % 4))

    def line_copy(m, d, src, dst):
        n = 96 + 3 * m + d - 1
        return remote(src, dst, ar_send.at[n], ar_recv.at[n], along((m + 2) % 3, d))

    def iteration(it, carry):
        lb[z, y] = d_ref[...].astype(BF16).reshape(2, 112, SIDE)
        for g_ in (0, 1):
            for h in (0, 1):
                send(h, g_)


        @pl.when(it > 0)
        def _():
            rp[...] = rp[...] - mm(qp[...], small[0])
            dp[...] = rp[...] + mm(dp[...], small[1])

        for k in range(3):
            for h in (0, 1):
                take(h, 0, (k,))
                send(h, k + 2)

        @pl.when(it == 0)
        def _():
            @pl.when(jnp.logical_not(fixed))
            def _():
                rows_in.start()

            @pl.when(fixed)
            def _():
                pltpu.make_async_copy(b_ref, rp, pm_recv.at[0]).start()

            load_a.wait()

        @pl.when(it > 0)
        def _():
            x_ref[...] += mm(dold[...], small[0])

        take(1, 1)
        all_products(z, True)
        for k in (1, 2):
            for g_ in (1, 2, 3, 4):
                take(0, g_, (k - 1,))
            take(1, k + 1)
            all_products(wrap(z + OFFS[k]), False)
        for g_ in (1, 2, 3, 4):
            take(0, g_, (2,))
        take(1, 4)

        last = wrap(z + 2)

        def finish(i, c_):
            j = 2 * part_of(i) + 1 - core
            product(last, j, False)
            core_copy(i).start()
            product(last, 2 * part_of(i) + core, False)
            return c_

        lax.fori_loop(0, 4, finish, 0)

        def chip_sum(i):
            core_copy(i).wait_recv()
            return part[2 * part_of(i) + core] + t1[i]

        for i in range(3):
            s3[i] = chip_sum(i).astype(WIRE)
            ring_copy(i).start()
        own = chip_sum(3)
        for h in (0, 1):
            for g_ in range(5):
                for e in range(3):
                    gather(h, g_, e, False).wait_send()
        for i in range(3):
            ring_copy(i).wait_recv()
        qp[...] = own + (t3[0].astype(F32) + t3[1].astype(F32) + t3[2].astype(F32))

        @pl.when(it == 0)
        def _():
            settle(rows_in)
            dp[...] = rp[...]

        image, res = qp[...], rp[...]
        theirs = pl.ds(pl.multiple_of((1 - core) * HALF, HALF), HALF)
        ours = pl.ds(pl.multiple_of(core * HALF, HALF), HALF)

        def swap(m):
            return remote(g.at[m, theirs], gt.at[m], ar_send.at[110 + m], ar_recv.at[110 + m], other_core)

        g[0] = mm_t(dp[...], image)
        swap(0).start()
        g[1] = mm_t(res, jnp.where(it == 0, res, image))
        swap(1).start()
        g[2] = mm_t(image, image)
        swap(2).start()
        for i in range(4):
            core_copy(i).wait_send()
        for i in range(3):
            ring_copy(i).wait_send()
        pending = []

        def each(m, fn):
            i, j = here[m], here[(m + 1) % 3]

            def step(k, c_):
                fn(k, i, j)
                return c_

            lax.fori_loop(1, 16, step, 0)

        def reduce_send(m, k, i, j):
            src = g0.at[m, wrap(i + k // 4), wrap(j + k % 4)]
            return plane_copy(0, m, k, src, u1.at[m, i, j])

        def spread_send(m, k, i, j):
            return plane_copy(48, m, k, h0.at[m, i, j], h0.at[m, i, j])

        for m in range(3):
            swap(m).wait_recv()
            g0[m] = (g[m, ours] + gt[m]).reshape(RING, RING, 8, SIDE)
            each(m, lambda k, i, j: reduce_send(m, k, i, j).start())
            i, j = here[m], here[(m + 1) % 3]
            u1[m, i, j] = g0[m, i, j]
        for m in range(3):
            def arrived(k, i, j):
                slot = u1.at[m, wrap(i - k // 4), wrap(j - k % 4)]
                plane_copy(0, m, k, slot, slot).wait_recv()

            each(m, arrived)
            g2[m] = jnp.sum(u1[m].reshape(16, 8, SIDE), axis=0)
            me = here[(m + 2) % 3]
            for d in (1, 3, 2):
                copy = line_copy(m, d, g2.at[m], u3.at[m, me])
                copy.start()
                pending.append(copy)
            u3[m, me] = g2[m]
        for m in range(3):
            me = here[(m + 2) % 3]
            for d in (1, 3, 2):
                slot = u3.at[m, wrap(me - d)]
                line_copy(m, d, slot, slot).wait_recv()
            h0[m, here[m], here[(m + 1) % 3]] = (u3[m, 0] + u3[m, 1]) + (u3[m, 2] + u3[m, 3])
            each(m, lambda k, i, j: spread_send(m, k, i, j).start())

        def join(m, half):
            return remote(gf.at[half, m], gf.at[half, m], ar_send.at[107 + m], ar_recv.at[107 + m], other_core)

        def land(m):
            def landed(k, i, j):
                slot = h0.at[m, wrap(i - k // 4), wrap(j - k % 4)]
                plane_copy(48, m, k, slot, slot).wait_recv()

            each(m, landed)
            gf[core, m] = h0[m].reshape(HALF, SIDE)
            join(m, core).start()

        def joined(m):
            join(m, 1 - core).wait_recv()
            full[m, :HALF] = gf[0, m]
            full[m, HALF:] = gf[1, m]

        first = it == 0
        later = it > 0
        land(0)

        @pl.when(first)
        def _():
            land(1)
            joined(1)
            norm[...] = full[1]

        owner_start(0)
        owner_start(1)
        raw = gf[core, 0, :, :HALF]
        head = eliminate(jnp.where(core == 0, 0.5 * (raw + raw.T), norm[:HALF, :HALF]), HALF)
        joined(0)
        raw = full[0]
        mat[...] = jnp.where(core == 0, 0.5 * (raw + raw.T), norm[...])
        t = mm(mat[HALF:, :HALF], head)
        corner = mat[HALF:, HALF:] - mm(t, mat[:HALF, HALF:])
        tri[...] = t
        work[...] = corner
        mat[:HALF, :HALF] = head
        tail = eliminate(work[...], HALF)
        t = tri[...]
        low = mm(tail, t)
        inv[core, :HALF, :HALF] = mat[:HALF, :HALF] + mm_t(t, low)
        inv[core, HALF:, :HALF] = -low
        inv[core, :HALF, HALF:] = -low.T
        inv[core, HALF:, HALF:] = tail
        share = remote(inv.at[core], inv.at[core], ar_send.at[106], ar_recv.at[106], other_core)
        share.start()
        pl.when(later)(lambda: land(1))
        land(2)
        remote(inv.at[1 - core], inv.at[1 - core], ar_send.at[106], ar_recv.at[106], other_core).wait_recv()
        alpha = mm(inv[0], norm[...])
        pl.when(later)(lambda: joined(1))
        joined(2)
        cross = jnp.where(first, full[0], full[1])
        for copy in pending:
            copy.wait_send()
        for m in range(3):
            swap(m).wait_send()
            join(m, core).wait_send()
            each(m, lambda k, i, j: reduce_send(m, k, i, j).wait_send())
            each(m, lambda k, i, j: spread_send(m, k, i, j).wait_send())
        fall = mm(cross, alpha)
        after = norm[...] - fall - fall.T + mm_t(alpha, mm(full[2], alpha))
        beta = mm(inv[1], after)
        norm[...] = after
        small[0] = alpha
        small[1] = beta

        dold[...] = d_ref[...]
        d_ref[...] = mm(d_ref[...], beta)
        for half in (0, 1):
            rows = pl.ds(112 * half, 112)
            settle(owner_copy(half))
            r_ref[rows] -= mm(q[rows], alpha)
            d_ref[rows] += r_ref[rows]
        share.wait_send()
        return carry

    lax.fori_loop(0, ITERS, iteration, 0)
    x_ref[...] += mm(dold[...], small[0])


def body(covariance, right_side):
    rows, cols = covariance.shape
    piece, side = right_side.shape
    vec = jax.ShapeDtypeStruct((piece, side), F32)
    vmem = pl.BlockSpec(memory_space=pltpu.VMEM)

    def f32(*shape):
        return pltpu.VMEM(shape, F32)

    def dma(n):
        return pltpu.SemaphoreType.DMA((n,))

    out = pl.pallas_call(
        kernel,
        out_shape=(vec, vec, vec),
        in_specs=[pl.BlockSpec(memory_space=pl.ANY), vmem],
        out_specs=(vmem, vmem, vmem),
        scratch_shapes=[
            pltpu.VMEM((8, piece, cols), BF16),
            pltpu.VMEM((4, 4, 2, piece // 2, side), BF16),
            f32(8, piece, side),
            f32(4, piece, side),
            pltpu.VMEM((3, piece, side), WIRE),
            pltpu.VMEM((3, piece, side), WIRE),
            f32(piece, side), f32(piece, side), f32(piece, side), f32(piece, side), f32(piece, side),
            f32(3, side, side), f32(3, HALF, side), f32(3, 4, 4, 8, side), f32(3, 4, 4, 8, side),
            f32(3, 8, side), f32(3, 4, 8, side), f32(3, 4, 4, 8, side), f32(2, 3, HALF, side),
            f32(side, side), f32(3, side, side), f32(2, side, side),
            f32(side, side), f32(HALF, HALF), f32(HALF, HALF), f32(2, side, side),
            pltpu.SemaphoreType.DMA,
            dma(30), dma(30), dma(7), dma(7), dma(3), dma(3), dma(113), dma(113),
        ],
        compiler_params=pltpu.CompilerParams(
            collective_id=0, has_side_effects=True, vmem_limit_bytes=60 * 1024 * 1024
        ),
    )(covariance.reshape(8, piece, cols), right_side)

    def hand_over(*refs):
        for src, dst in zip(refs[:3], refs[3:]):
            dst[...] = src[...]

    return pl.pallas_call(hand_over, out_shape=(vec, vec, vec))(*out)


def solution(mesh):
    spec = P(("col", "row"), None)
    return jax.shard_map(
        body,
        mesh=mesh,
        in_specs=(P("row", "col"), spec),
        out_specs=(spec, spec, spec),
        check_vma=False,
    )
```
